256 devices in a mesh: dp: 8 (over y, core), owner: 32 (over x, z).
Axes of the slice: x: 4, y: 4, z: 8, core: 2. Of those that a mesh axis runs over, the one named last changes fastest.
Arguments:
- tokens: bfloat16 [32768, 8192], P(('dp', 'owner')), may hold values from -6 to 6
- adapter_index: int32 [32768, 1], P(('dp', 'owner')), may hold values from 0 to 63; in each aligned block of 128 rows (0 to 127, 128 to 255, ...) at most 3 rows name the same one
- query_cotangent: bfloat16 [32768, 8192], P(('dp', 'owner')), may hold values from -6 to 6
- value_cotangent: bfloat16 [32768, 1024], P(('dp', 'owner')), may hold values from -6 to 6
- shrink: bfloat16 [64, 2, 64, 8192], P('owner', None, None, 'dp'), may hold values from -0.0625 to 0.0625
- query_expand: bfloat16 [64, 64, 8192], P('owner', None, 'dp'), may hold values from -0.75 to 0.75
- value_expand: bfloat16 [64, 64, 1024], P('owner', None, 'dp'), may hold values from -0.75 to 0.75
Outputs:
- query_delta: bfloat16 [32768, 8192], P(('dp', 'owner'))
- value_delta: bfloat16 [32768, 1024], P(('dp', 'owner'))
- token_gradient: bfloat16 [32768, 8192], P(('dp', 'owner'))
- shrink_gradient: float32 [64, 2, 64, 8192], P('owner', None, None, 'dp')
- query_gradient: float32 [64, 64, 8192], P('owner', None, 'dp')
- value_gradient: float32 [64, 64, 1024], P('owner', None, 'dp')
The draws below stay inside these ranges and needn't reach their ends.
Inputs may be any that keep to these rules, and one draw needn't show every extreme that they name: `adapter_index`: within each device's aligned block of 128 tokens no adapter is named by more than 3 tokens, a bound that some block reaches.
All inputs are finite; a program needn't handle non-finite values.
Results may differ from the reference program's by a relative error of at most 0.0049.
Values may be sent and summed in bfloat16 or wider, within the bound.
No kernel may reach another device: no remote copies, remote signals or barrier semaphores. Data moves between devices by JAX's collectives and lax.ppermute only.
A program may use at most 128 MiB of HBM per device.

```python
import math
import jax
import jax.numpy as jnp
import numpy as np
from jax import lax

D = 8192
DV = 1024
R = 64
TOK_DEV = 128
ADAPTERS = 64
CAP = 3
TOKENS = 32768
N_DP = 8
N_OWNER = 32


def levels(stream_key, shape, split, least, top_value):
    gain, own = 1.0, jax.random.fold_in(stream_key, 6)
    for dim, blocks in split:
        draws = jnp.exp(jax.random.uniform(jax.random.fold_in(own, dim), (blocks,), jnp.float32, least / len(split), top_value / len(split)))
        gain = gain * jnp.repeat(draws, shape[dim] // blocks).reshape([-1 if axis == dim else 1 for axis in range(len(shape))])
    return gain


def assign_block(stream_key, own, number, rows, amount, top, reach, skew):
    ranking = jax.random.permutation(stream_key, amount)
    packed, ordinary = portions_of(amount, rows * top, reach, skew, True), portions_of(amount, rows * top, reach, skew, False)
    places = jnp.arange(amount)

    def named(tallies, rotation):
        used = int((tallies > 0).sum())
        fixed = max(1, used // 4)
        moved = fixed + (places - fixed + rotation * (used - fixed)) % max(1, amount - fixed)
        return jnp.zeros((amount,), jnp.int32).at[ranking[jnp.where(places < fixed, places, moved)]].set(jnp.asarray(tallies, jnp.int32))

    tallies = jnp.where(number % 4 == 0, named(packed, number // 4), named(ordinary, number - number // 4 - 1))
    mixed = jax.random.permutation(jax.random.fold_in(own, 3), amount)
    donor, sink = mixed[0:amount // 2 * 2:2], mixed[1:amount // 2 * 2:2]
    margin = jnp.minimum(tallies[donor] - 1, reach - tallies[sink]) // 2
    margin = jnp.where((donor == ranking[0]) | (sink == ranking[0]) | (tallies[sink] == 0), 0, jnp.maximum(margin, 0))
    moved = jax.random.randint(jax.random.fold_in(own, 4), (amount // 2,), 0, 1 << 20) % (margin + 1)
    tallies = tallies.at[donor].add(-moved).at[sink].add(moved)
    labels = jnp.searchsorted(jnp.cumsum(tallies), jnp.arange(rows * top), side="right").astype(jnp.int32)
    grid = labels.reshape(top, rows).T
    grid = grid[jax.random.permutation(jax.random.fold_in(own, 1), rows)]
    rotation = jax.random.randint(jax.random.fold_in(own, 2), (rows, 1), 0, top)
    return jnp.take_along_axis(grid, (jnp.arange(top)[None, :] + rotation) % top, axis=1)


def portions_of(count, total, reach, skew, full):
    weights = [(1 << 20) // math.isqrt(rank ** skew) + 1 for rank in range(1, count + 1)]
    largest = reach if full else min(reach, max(-(-total // count), total * weights[0] // sum(weights)))
    least = 1 if total - largest >= count - 1 else 0
    given, spare = [largest] + [least] * (count - 1), total - largest - least * (count - 1)
    while spare > 0:
        candidates = [i for i in range(1, count) if given[i] < largest] or [i for i in range(1, count) if given[i] < reach]
        whole, remaining = sum([weights[i] for i in candidates]), spare
        for i in candidates:
            extra = min(reach - given[i], max(1, remaining * weights[i] // whole), spare)
            given[i] = given[i] + extra
            spare = spare - extra
    return np.array(given)


def scatter_about(rng, dims, width, reach, cuts=(), kind=jnp.bfloat16):
    values = width * jax.random.normal(rng, dims, jnp.float32)
    if cuts:
        values = values * levels(rng, dims, cuts, -0.22, 0.18)
    return jnp.clip(values, -reach, reach).astype(kind)


def setup_inputs(seed: int = 0) -> dict:
    key_of = jax.random.split(jax.random.key(seed), 8)
    tokens = scatter_about(key_of[0], (TOKENS, D), 1.0, 6.0, ((0, 256),))
    adapter_index_keys = jax.random.split(jax.random.fold_in(key_of[1], 1), TOKENS // TOK_DEV)
    adapter_index_turns = jax.random.permutation(jax.random.fold_in(key_of[1], 3), TOKENS // TOK_DEV)
    adapter_index = jax.vmap(lambda own, number: assign_block(jax.random.fold_in(key_of[1], 2), own, number, TOK_DEV, ADAPTERS, 1, CAP, 2))(adapter_index_keys, adapter_index_turns).reshape((TOKENS, 1))
    query_cotangent = scatter_about(key_of[2], (TOKENS, D), 1.0, 6.0, ((0, 256),))
    value_cotangent = scatter_about(key_of[3], (TOKENS, DV), 1.0, 6.0, ((0, 256),))
    shrink = scatter_about(key_of[4], (ADAPTERS, 2, R, D), D ** -0.5, 0.0625, ((0, 32), (3, 8)))
    query_expand = scatter_about(key_of[5], (ADAPTERS, R, D), R ** -0.5, 0.75, ((0, 32), (2, 8)))
    value_expand = scatter_about(key_of[6], (ADAPTERS, R, DV), R ** -0.5, 0.75, ((0, 32), (2, 8)))
    return dict(tokens=tokens, adapter_index=adapter_index, query_cotangent=query_cotangent, value_cotangent=value_cotangent, shrink=shrink, query_expand=query_expand, value_expand=value_expand)


adapter_scale_factor = 0.5


def reference(tokens, adapter_index, query_cotangent, value_cotangent, shrink, query_expand, value_expand):
    adapter_of = adapter_index[:, 0].astype(jnp.int32)
    tok_count = tokens.shape[0]
    adapter_count = shrink.shape[0]
    most_rows = N_DP * N_OWNER * CAP
    onehot = (adapter_of[:, None] == jnp.arange(adapter_count, dtype=jnp.int32)[None, :]).astype(jnp.int32)
    earlier = jnp.cumsum(onehot, axis=0) - onehot
    ordinal = jnp.sum(earlier * onehot, axis=1).astype(jnp.int32)
    table = jnp.full((adapter_count, most_rows), tok_count, jnp.int32)
    table = table.at[adapter_of, ordinal].set(jnp.arange(tok_count, dtype=jnp.int32))

    def one_adapter(carry, inputs):
        query_all, value_all, token_all = carry
        rows, down_pair, query_up_weight, value_up_weight = inputs
        picked = jnp.take(tokens, rows, axis=0, mode="fill", fill_value=0)
        selected_query = jnp.take(query_cotangent, rows, axis=0, mode="fill", fill_value=0)
        selected_value = jnp.take(value_cotangent, rows, axis=0, mode="fill", fill_value=0)
        reduced_query = jnp.dot(picked, down_pair[0].T, preferred_element_type=jnp.float32).astype(jnp.bfloat16)
        reduced_value = jnp.dot(picked, down_pair[1].T, preferred_element_type=jnp.float32).astype(jnp.bfloat16)
        query_result = (adapter_scale_factor * jnp.dot(reduced_query, query_up_weight, preferred_element_type=jnp.float32)).astype(jnp.bfloat16)
        value_result = (adapter_scale_factor * jnp.dot(reduced_value, value_up_weight, preferred_element_type=jnp.float32)).astype(jnp.bfloat16)
        backprop_query_rows = (adapter_scale_factor * jnp.dot(selected_query, query_up_weight.T, preferred_element_type=jnp.float32)).astype(jnp.bfloat16)
        backprop_value_rows = (adapter_scale_factor * jnp.dot(selected_value, value_up_weight.T, preferred_element_type=jnp.float32)).astype(jnp.bfloat16)
        token_out = (jnp.dot(backprop_query_rows, down_pair[0], preferred_element_type=jnp.float32)
                     + jnp.dot(backprop_value_rows, down_pair[1], preferred_element_type=jnp.float32)).astype(jnp.bfloat16)
        grad_down = jnp.stack([jnp.dot(backprop_query_rows.T, picked, preferred_element_type=jnp.float32),
                               jnp.dot(backprop_value_rows.T, picked, preferred_element_type=jnp.float32)], axis=0)
        query_weight_gradient = adapter_scale_factor * jnp.dot(reduced_query.T, selected_query, preferred_element_type=jnp.float32)
        value_weight_gradient = adapter_scale_factor * jnp.dot(reduced_value.T, selected_value, preferred_element_type=jnp.float32)
        query_all = query_all.at[rows].set(query_result, mode="drop")
        value_all = value_all.at[rows].set(value_result, mode="drop")
        token_all = token_all.at[rows].set(token_out, mode="drop")
        return (query_all, value_all, token_all), (grad_down, query_weight_gradient, value_weight_gradient)

    start = (jnp.zeros(query_cotangent.shape, jnp.bfloat16), jnp.zeros(value_cotangent.shape, jnp.bfloat16), jnp.zeros(tokens.shape, jnp.bfloat16))
    outputs, gradients = lax.scan(one_adapter, start, (table, shrink, query_expand, value_expand))
    return outputs[0], outputs[1], outputs[2], gradients[0], gradients[1], gradients[2]
```

```python
import jax
import jax.numpy as jnp
from jax import lax
from jax.experimental import pallas as pl
from jax.experimental.pallas import tpu as pltpu
from jax.sharding import Mesh, PartitionSpec as P

SCALE = 0.5
F32 = jnp.float32
BF16 = jnp.bfloat16
CAP = 3
TILE = 16
PER = 5
TILES = 3
GROUP = PER * TILES + 1
SLOTS = TILE * TILES


def iota(shape, dim):
    return lax.broadcasted_iota(jnp.int32, shape, dim)


def slot_of(adapter, ordinal):
    group = adapter >> 4
    inner = adapter & 15
    tile = (inner >= PER).astype(jnp.int32) + (inner >= 2 * PER).astype(jnp.int32)
    spot = jnp.where(
        inner == GROUP - 1, ordinal * TILE + TILE - 1, tile * TILE + (inner - tile * PER) * CAP + ordinal
    )
    return group * SLOTS + spot


def as_row(column):
    n = column.shape[0]
    return jnp.sum(jnp.where(iota((n, n), 0) == iota((n, n), 1), column, 0), axis=0, keepdims=True)


def placing_rows(adapter, slots):
    n = adapter.shape[0]
    row = as_row(adapter)
    same = (adapter == row) & (iota((n, n), 0) < iota((n, n), 1))
    target = slot_of(row, jnp.sum(same.astype(jnp.int32), axis=0, keepdims=True))
    return (iota((slots, n), 0) == target).astype(F32).astype(BF16)


def placing_columns(adapter, slots):
    n = adapter.shape[0]
    row = as_row(adapter)
    same = (adapter == row) & (iota((n, n), 1) < iota((n, n), 0))
    target = slot_of(adapter, jnp.sum(same.astype(jnp.int32), axis=1, keepdims=True))
    return (iota((n, slots), 1) == target).astype(F32).astype(BF16)


def row_block(rows):
    inner = iota((rows, 128), 0) & (TILE - 1)
    block = jnp.zeros((rows, 128), jnp.int32)
    for k in range(1, PER + 1):
        block = block + (inner >= CAP * k).astype(jnp.int32)
    return block


def pair_mask(rows, pair):
    half = (iota((rows, 128), 1) >= 64).astype(jnp.int32)
    return row_block(rows) == 2 * pair + half


def params():
    return pltpu.CompilerParams(vmem_limit_bytes=56 << 20)


def cost(flops, moved):
    return pl.CostEstimate(flops=flops, bytes_accessed=moved, transcendentals=0)


def place(adapter, values, parts, slots, name):
    n = adapter.shape[0]
    widths = [v.shape[1] // parts for v in values]
    total = sum(widths)

    def kernel(a_ref, *refs):
        ins, o_ref, p_ref = refs[: len(values)], refs[-2], refs[-1]

        @pl.when(pl.program_id(0) == 0)
        def _():
            p_ref[...] = placing_rows(a_ref[...], slots)

        at = 0
        for v_ref, width in zip(ins, widths):
            o_ref[0, :, at : at + width] = jnp.dot(
                p_ref[...], v_ref[...], preferred_element_type=F32
            ).astype(BF16)
            at += width

    return pl.pallas_call(
        kernel,
        grid=(parts,),
        in_specs=[pl.BlockSpec((n, 1), lambda j: (0, 0))]
        + [pl.BlockSpec((n, width), lambda j: (0, j)) for width in widths],
        out_specs=pl.BlockSpec((1, slots, total), lambda j: (j, 0, 0)),
        out_shape=jax.ShapeDtypeStruct((parts, slots, total), BF16),
        scratch_shapes=[pltpu.VMEM((slots, n), BF16)],
        compiler_params=params(),
        cost_estimate=cost(2 * slots * n * total * parts, 2 * parts * total * (n + slots)),
        name=name,
    )(adapter, *values)


def collect(adapter, moved, widths, name):
    n = adapter.shape[0]
    parts, slots, total = moved.shape

    def kernel(a_ref, m_ref, *refs):
        outs, p_ref = refs[:-1], refs[-1]

        @pl.when(pl.program_id(0) == 0)
        def _():
            p_ref[...] = placing_columns(a_ref[...], slots)

        at = 0
        for o_ref, width in zip(outs, widths):
            o_ref[...] = jnp.dot(
                p_ref[...], m_ref[0, :, at : at + width], preferred_element_type=F32
            ).astype(BF16)
            at += width

    return pl.pallas_call(
        kernel,
        grid=(parts,),
        in_specs=[
            pl.BlockSpec((n, 1), lambda j: (0, 0)),
            pl.BlockSpec((1, slots, total), lambda j: (j, 0, 0)),
        ],
        out_specs=[pl.BlockSpec((n, width), lambda j: (0, j)) for width in widths],
        out_shape=[jax.ShapeDtypeStruct((n, width * parts), BF16) for width in widths],
        scratch_shapes=[pltpu.VMEM((n, slots), BF16)],
        compiler_params=params(),
        cost_estimate=cost(2 * slots * n * total * parts, 2 * parts * total * (n + slots)),
        name=name,
    )(adapter, moved)


def take_weights(w_ref, pick_ref, t):
    rank = w_ref.shape[1]
    width = w_ref.shape[2]
    pick_ref[: PER * rank, :] = w_ref[pl.ds(PER * t, PER)].reshape(PER * rank, width)
    pick_ref[PER * rank :, :] = w_ref[GROUP - 1]


def by_tile(kernel, ins, out, scratch, flops, name):
    def spec(shape):
        if shape[1] == SLOTS:
            return pl.BlockSpec((shape[0], TILE, shape[2]), lambda t: (0, t, 0))
        return pl.BlockSpec(shape, lambda t: (0, 0, 0))

    moved = sum(v.size * v.dtype.itemsize for v in ins) + out.size * out.dtype.itemsize
    return pl.pallas_call(
        kernel,
        grid=(TILES,),
        in_specs=[spec(v.shape) for v in ins],
        out_specs=spec(out.shape),
        out_shape=out,
        scratch_shapes=scratch,
        compiler_params=params(),
        cost_estimate=cost(flops, moved),
        name=name,
    )(*ins)


def lowered_part(rows, shrink):
    sources, _, width = rows.shape
    count, rank = sources * TILE, shrink.shape[1]

    def kernel(x_ref, w_ref, o_ref, pick_ref):
        take_weights(w_ref, pick_ref, pl.program_id(0))
        dense = lax.dot_general(
            x_ref[...].reshape(count, width),
            pick_ref[...],
            (((1,), (1,)), ((), ())),
            preferred_element_type=F32,
        )
        block = row_block(count)
        total = jnp.zeros((count, rank), F32)
        for b in range(PER + 1):
            total = total + jnp.where(block == b, dense[:, b * rank : (b + 1) * rank], 0.0)
        o_ref[...] = total.reshape(sources, TILE, rank)

    return by_tile(
        kernel,
        (rows, shrink),
        jax.ShapeDtypeStruct((sources, SLOTS, rank), F32),
        [pltpu.VMEM(((PER + 1) * rank, width), BF16)],
        2 * TILES * count * (PER + 1) * rank * width,
        "lowered_part",
    )


def backward_part(rows, expand, split):
    sources, _, width = rows.shape
    count, rank = sources * TILE, expand.shape[1]

    def kernel(x_ref, w_ref, o_ref, pick_ref):
        take_weights(w_ref, pick_ref, pl.program_id(0))
        x = x_ref[...].reshape(count, width)

        def part(lo, hi):
            dense = lax.dot_general(
                x[:, lo:hi], pick_ref[:, lo:hi], (((1,), (1,)), ((), ())), preferred_element_type=F32
            )
            total = jnp.zeros((count, 2 * rank), F32)
            for p in range((PER + 1) // 2):
                piece = dense[:, 2 * rank * p : 2 * rank * (p + 1)]
                total = total + jnp.where(pair_mask(count, p), piece, 0.0)
            return total + pltpu.roll(total, rank, 1)

        first = iota((count, 2 * rank), 1) < rank
        both = jnp.where(first, part(0, split), part(split, width))
        o_ref[...] = both.reshape(sources, TILE, 2 * rank)

    return by_tile(
        kernel,
        (rows, expand),
        jax.ShapeDtypeStruct((sources, SLOTS, 2 * rank), F32),
        [pltpu.VMEM(((PER + 1) * rank, width), BF16)],
        2 * TILES * count * (PER + 1) * rank * width,
        "backward_part",
    )


def spread_pairs(values, count, rank):
    held = values.reshape(count, 2 * rank).astype(F32)
    turned = pltpu.roll(held, rank, 1)
    first = iota((count, 2 * rank), 1) < rank
    halves = (jnp.where(first, held, turned), jnp.where(first, turned, held))
    return [
        jnp.concatenate(
            [jnp.where(pair_mask(count, p), half, 0.0) for p in range((PER + 1) // 2)], axis=1
        ).astype(BF16)
        for half in halves
    ]


def spread_blocks(values, count, rank):
    held = values.reshape(count, rank).astype(F32)
    block = row_block(count)
    return jnp.concatenate(
        [jnp.where(block == b, held, 0.0) for b in range(PER + 1)], axis=1
    ).astype(BF16)


def expand_rows(lowered, expand, split):
    sources = lowered.shape[0]
    count, rank, width = sources * TILE, expand.shape[1], expand.shape[2]

    def kernel(l_ref, w_ref, o_ref, pick_ref):
        take_weights(w_ref, pick_ref, pl.program_id(0))
        halves = spread_pairs(l_ref[...], count, rank)
        for half, lo, hi in zip(halves, (0, split), (split, width)):
            result = SCALE * jnp.dot(half, pick_ref[:, lo:hi], preferred_element_type=F32)
            o_ref[:, :, lo:hi] = result.astype(BF16).reshape(sources, TILE, hi - lo)

    return by_tile(
        kernel,
        (lowered, expand),
        jax.ShapeDtypeStruct((sources, SLOTS, width), BF16),
        [pltpu.VMEM(((PER + 1) * rank, width), BF16)],
        2 * TILES * count * (PER + 1) * rank * width,
        "expand_rows",
    )


def token_rows(backward, shrink):
    sources = backward.shape[0]
    count, rank, width = sources * TILE, shrink.shape[1], shrink.shape[2]

    def kernel(b_ref, w_ref, o_ref, pick_ref):
        take_weights(w_ref, pick_ref, pl.program_id(0))
        wide = spread_blocks(b_ref[...], count, rank)
        result = jnp.dot(wide, pick_ref[...], preferred_element_type=F32)
        o_ref[...] = result.astype(BF16).reshape(sources, TILE, width)

    return by_tile(
        kernel,
        (backward, shrink),
        jax.ShapeDtypeStruct((sources, SLOTS, width), BF16),
        [pltpu.VMEM(((PER + 1) * rank, width), BF16)],
        2 * TILES * count * (PER + 1) * rank * width,
        "token_rows",
    )


def put_gradient(o_ref, last_ref, pieces, rank, lo, hi):
    t = pl.program_id(0)
    o_ref[pl.ds(PER * t, PER), :, lo:hi] = (
        pieces[: PER * rank].astype(BF16).reshape(PER, rank, hi - lo)
    )
    last = pieces[PER * rank :]

    @pl.when(t == 0)
    def _():
        last_ref[:, lo:hi] = last

    @pl.when(t > 0)
    def _():
        last_ref[:, lo:hi] = last_ref[:, lo:hi] + last

    @pl.when(t == TILES - 1)
    def _():
        o_ref[GROUP - 1, :, lo:hi] = last_ref[:, lo:hi].astype(BF16)


def expand_gradient(lowered, rows, rank, split):
    sources, _, width = rows.shape
    count = sources * TILE

    def kernel(l_ref, x_ref, o_ref, last_ref):
        x = x_ref[...].reshape(count, width)
        halves = spread_pairs(l_ref[...], count, rank)
        for half, lo, hi in zip(halves, (0, split), (split, width)):
            pieces = SCALE * lax.dot_general(
                half, x[:, lo:hi], (((0,), (0,)), ((), ())), preferred_element_type=F32
            )
            put_gradient(o_ref, last_ref, pieces, rank, lo, hi)

    return by_tile(
        kernel,
        (lowered, rows),
        jax.ShapeDtypeStruct((GROUP, rank, width), BF16),
        [pltpu.VMEM((rank, width), F32)],
        2 * TILES * count * (PER + 1) * rank * width,
        "expand_gradient",
    )


def shrink_gradient(backward, rows):
    sources, _, width = rows.shape
    count, rank = sources * TILE, backward.shape[2]

    def kernel(b_ref, x_ref, o_ref, last_ref):
        wide = spread_blocks(b_ref[...], count, rank)
        pieces = lax.dot_general(
            wide,
            x_ref[...].reshape(count, width),
            (((0,), (0,)), ((), ())),
            preferred_element_type=F32,
        )
        put_gradient(o_ref, last_ref, pieces, rank, 0, width)

    return by_tile(
        kernel,
        (backward, rows),
        jax.ShapeDtypeStruct((GROUP, rank, width), BF16),
        [pltpu.VMEM((rank, width), F32)],
        2 * TILES * count * (PER + 1) * rank * width,
        "shrink_gradient",
    )


ROUTE = ("y", "c", "x")
PARTS = ("y", "c")


def exchange(values, axes):
    return lax.all_to_all(values, axes, 0, 0, tiled=True)


def combine(partial, factor, parts):
    sources, slots, rank = partial.shape
    pieces = exchange(partial.reshape(parts, sources * slots // parts, rank), PARTS)
    total = (factor * jnp.sum(pieces.reshape(parts, -1, rank), axis=0)).astype(BF16)
    return lax.all_gather(total, PARTS, axis=0, tiled=True).reshape(sources, slots, rank)


def body(tokens, adapter_index, query_cotangent, value_cotangent, shrink, query_expand, value_expand):
    parts = lax.axis_size(PARTS)
    sources = lax.axis_size(ROUTE)
    groups = sources // parts
    slots = groups * SLOTS
    local, kinds, rank, width = shrink.shape
    value_width = value_expand.shape[2]
    both = width + value_width

    whole_shrink = lax.all_gather(shrink.reshape(local, kinds * rank, width), "z", axis=0, tiled=True)
    whole_expand = lax.all_gather(
        jnp.concatenate([query_expand, value_expand], axis=2), "z", axis=0, tiled=True
    )

    sent_tokens = place(adapter_index, (tokens,), parts, slots, "place_tokens")
    rows_tokens = exchange(sent_tokens.reshape(sources, SLOTS, width), ROUTE)
    sent_both = place(adapter_index, (query_cotangent, value_cotangent), parts, slots, "place_cotangents")
    rows_both = exchange(sent_both.reshape(sources, SLOTS, both), ROUTE)

    lowered = combine(lowered_part(rows_tokens, whole_shrink), 1.0, parts)
    out_both = exchange(expand_rows(lowered, whole_expand, width), ROUTE)
    backward = combine(backward_part(rows_both, whole_expand, width), SCALE, parts)
    out_tokens = exchange(token_rows(backward, whole_shrink), ROUTE)

    grad_expand = lax.psum_scatter(
        expand_gradient(lowered, rows_both, rank, width), "z", scatter_dimension=0, tiled=True
    ).astype(F32)
    grad_shrink = lax.psum_scatter(
        shrink_gradient(backward, rows_tokens), "z", scatter_dimension=0, tiled=True
    ).astype(F32)

    query_delta, value_delta = collect(
        adapter_index, out_both.reshape(parts, slots, both), (width, value_width), "collect_deltas"
    )
    (token_gradient,) = collect(
        adapter_index, out_tokens.reshape(parts, slots, width), (width,), "collect_tokens"
    )
    return (
        query_delta,
        value_delta,
        token_gradient,
        grad_shrink.reshape(local, kinds, rank, width),
        grad_expand[:, :, :width],
        grad_expand[:, :, width:],
    )


def solution(mesh):
    grid = Mesh(mesh.devices.reshape(4, 2, 4, 8), ("y", "c", "x", "z"))
    rows = P(("y", "c", "x", "z"), None)
    return jax.shard_map(
        body,
        mesh=grid,
        in_specs=(
            rows,
            rows,
            rows,
            rows,
            P(("x", "z"), None, None, PARTS),
            P(("x", "z"), None, PARTS),
            P(("x", "z"), None, PARTS),
        ),
        out_specs=(
            rows,
            rows,
            rows,
            P(("x", "z"), None, None, PARTS),
            P(("x", "z"), None, PARTS),
            P(("x", "z"), None, PARTS),
        ),
        check_vma=False,
    )
```

```python
import jax
import jax.numpy as jnp
from jax import lax
from jax.experimental import pallas as pl
from jax.experimental.pallas import tpu as pltpu
from jax.sharding import Mesh, PartitionSpec as P


SCALE = 0.5
F32 = jnp.float32
BF16 = jnp.bfloat16
CAP = 3
PAIR = 2
CUTS = 8
BLOCKS = CUTS * PAIR
SLOTS = BLOCKS * CAP
TILE = 16
TILES = SLOTS // TILE
STEP = 5
HELD = STEP + 1
NEAR = 4


def iota(shape, dim):
    return lax.broadcasted_iota(jnp.int32, shape, dim)


def target_of(adapter, ordinal):
    dest = ((adapter >> 1) & 7) * 4 + (adapter >> 4)
    return dest * SLOTS + (adapter & 1) * CAP + ordinal


def as_row(column):
    n = column.shape[0]
    return jnp.sum(jnp.where(iota((n, n), 0) == iota((n, n), 1), column, 0), axis=0, keepdims=True)


def target_row(adapter):
    n = adapter.shape[0]
    row = as_row(adapter)
    same = (adapter == row) & (iota((n, n), 0) < iota((n, n), 1))
    return target_of(row, jnp.sum(same.astype(jnp.int32), axis=0, keepdims=True))


def target_column(adapter):
    n = adapter.shape[0]
    same = (adapter == as_row(adapter)) & (iota((n, n), 1) < iota((n, n), 0))
    return target_of(adapter, jnp.sum(same.astype(jnp.int32), axis=1, keepdims=True))


def slot_at(index, t):
    return (index >> 4) * SLOTS + t * TILE + (index & (TILE - 1))


def row_block(rows, t):
    inner = (iota((rows, 128), 0) & (TILE - 1)) + t
    block = jnp.zeros((rows, 128), jnp.int32)
    for k in range(1, HELD):
        block = block + (inner >= CAP * k).astype(jnp.int32)
    return block


def pair_of(block, pair):
    half = (iota(block.shape, 1) >= 64).astype(jnp.int32)
    return block == 2 * pair + half


def params():
    return pltpu.CompilerParams(vmem_limit_bytes=30 << 20)


def cost(flops, moved):
    return pl.CostEstimate(flops=flops, bytes_accessed=moved, transcendentals=0)


def place(adapter, values, sources):
    n = adapter.shape[0]
    widths = [v.shape[1] // CUTS for v in values]
    total = sum(widths)
    count = sources * TILE

    def kernel(a_ref, *refs):
        ins, o_ref = refs[:-1], refs[-1]
        t = pl.program_id(0)
        first = target_row(a_ref[...])
        slot = slot_at(iota((count, n), 0), t)
        spots = jnp.concatenate(
            [slot == first + PAIR * CAP * (2 * t + near) for near in range(NEAR)], axis=1
        )
        spots = spots.astype(F32).astype(BF16)
        at = 0
        for v_ref, width in zip(ins, widths):
            begin = pl.multiple_of(2 * t * width, 128)
            held = v_ref[:, pl.ds(begin, NEAR * width)]
            held = jnp.concatenate(
                [held[:, near * width : (near + 1) * width] for near in range(NEAR)], axis=0
            )
            moved = jnp.dot(spots, held, preferred_element_type=F32).astype(BF16)
            o_ref[:, :, at : at + width] = moved.reshape(sources, TILE, width)
            at += width

    return pl.pallas_call(
        kernel,
        grid=(TILES,),
        in_specs=[pl.BlockSpec((n, 1), lambda t: (0, 0))]
        + [pl.BlockSpec(v.shape, lambda t: (0, 0)) for v in values],
        out_specs=pl.BlockSpec((sources, TILE, total), lambda t: (0, t, 0)),
        out_shape=jax.ShapeDtypeStruct((sources, SLOTS, total), BF16),
        compiler_params=params(),
        cost_estimate=cost(2 * sources * SLOTS * n * NEAR * total, 2 * total * (CUTS * n + sources * SLOTS)),
    )(adapter, *values)


def collect(adapter, moved, widths):
    n = adapter.shape[0]
    sources, _, total = moved.shape
    count = sources * TILE

    def kernel(a_ref, m_ref, *outs):
        t = pl.program_id(0)
        first = target_column(a_ref[...])
        slot = slot_at(iota((n, count), 1), t)
        spots = jnp.concatenate(
            [slot == first + PAIR * CAP * (2 * t + near) for near in range(NEAR)], axis=0
        )
        spots = spots.astype(F32).astype(BF16)
        at = 0
        for o_ref, width in zip(outs, widths):
            found = jnp.dot(
                spots, m_ref[:, :, at : at + width].reshape(count, width), preferred_element_type=F32
            )
            for near in range(NEAR):
                here = pl.ds(pl.multiple_of((2 * t + near) * width, 128), width)
                piece = found[near * n : (near + 1) * n]
                if near < 2:
                    piece = piece + jnp.where(t > 0, o_ref[:, here].astype(F32), 0.0)
                o_ref[:, here] = piece.astype(BF16)
            at += width

    return pl.pallas_call(
        kernel,
        grid=(TILES,),
        in_specs=[
            pl.BlockSpec((n, 1), lambda t: (0, 0)),
            pl.BlockSpec((sources, TILE, total), lambda t: (0, t, 0)),
        ],
        out_specs=[pl.BlockSpec((n, width * CUTS), lambda t: (0, 0)) for width in widths],
        out_shape=[jax.ShapeDtypeStruct((n, width * CUTS), BF16) for width in widths],
        compiler_params=params(),
        cost_estimate=cost(2 * sources * SLOTS * n * NEAR * total, 2 * total * (CUTS * n + sources * SLOTS)),
    )(adapter, moved)


def held_weights(w_ref, t):
    _, rank, width = w_ref.shape
    return w_ref[pl.ds(STEP * t, HELD)].reshape(HELD * rank, width)


def by_tile(kernel, ins, out, scratch, flops, whole_out=False):
    def spec(shape):
        if shape[1] == SLOTS:
            return pl.BlockSpec((shape[0], TILE, shape[2]), lambda t: (0, t, 0))
        return pl.BlockSpec(shape, lambda t: (0, 0, 0))

    moved = sum(v.size * v.dtype.itemsize for v in ins) + out.size * out.dtype.itemsize
    return pl.pallas_call(
        kernel,
        grid=(TILES,),
        in_specs=[spec(v.shape) for v in ins],
        out_specs=pl.BlockSpec(out.shape, lambda t: (0, 0, 0)) if whole_out else spec(out.shape),
        out_shape=out,
        scratch_shapes=scratch,
        compiler_params=params(),
        cost_estimate=cost(flops, moved),
    )(*ins)


def sum_slices(part_ref, o_ref, factor):
    half = SLOTS // 2
    total = part_ref[:, :half, :] + part_ref[:, half:, :]
    total = total + pltpu.roll(total, half // 2, 1)
    total = total + pltpu.roll(total, half // 4, 1)
    o_ref[...] = (factor * jnp.concatenate([total, total], axis=1)).astype(BF16)


def keep_part(part_ref, t, part):
    for tile in range(TILES):

        @pl.when(t == tile)
        def _(tile=tile):
            part_ref[:, tile * TILE : (tile + 1) * TILE, :] = part


def lowered_rows(rows, shrink):
    sources, _, width = rows.shape
    count, rank = sources * TILE, shrink.shape[1]

    def kernel(x_ref, w_ref, o_ref, part_ref):
        t = pl.program_id(0)
        dense = lax.dot_general(
            x_ref[...].reshape(count, width),
            held_weights(w_ref, t),
            (((1,), (1,)), ((), ())),
            preferred_element_type=F32,
        )
        block = row_block(count, t)
        total = jnp.zeros((count, rank), F32)
        for b in range(HELD):
            total = total + jnp.where(block == b, dense[:, b * rank : (b + 1) * rank], 0.0)
        keep_part(part_ref, t, total.reshape(sources, TILE, rank))

        @pl.when(t == TILES - 1)
        def _():
            sum_slices(part_ref, o_ref, 1.0)

    return by_tile(
        kernel,
        (rows, shrink),
        jax.ShapeDtypeStruct((sources, SLOTS, rank), BF16),
        [pltpu.VMEM((sources, SLOTS, rank), F32)],
        2 * TILES * count * HELD * rank * width,
        whole_out=True,
    )


def backward_rows(rows, expand, split):
    sources, _, width = rows.shape
    count, rank = sources * TILE, expand.shape[1]

    def kernel(x_ref, w_ref, o_ref, part_ref):
        t = pl.program_id(0)
        x = x_ref[...].reshape(count, width)
        w = held_weights(w_ref, t)
        block = row_block(count, t)

        def part(lo, hi):
            dense = lax.dot_general(
                x[:, lo:hi], w[:, lo:hi], (((1,), (1,)), ((), ())), preferred_element_type=F32
            )
            total = jnp.zeros((count, 2 * rank), F32)
            for p in range(HELD // 2):
                piece = dense[:, 2 * rank * p : 2 * rank * (p + 1)]
                total = total + jnp.where(pair_of(block, p), piece, 0.0)
            return total + pltpu.roll(total, rank, 1)

        first = iota((count, 2 * rank), 1) < rank
        both = jnp.where(first, part(0, split), part(split, width))
        keep_part(part_ref, t, both.reshape(sources, TILE, 2 * rank))

        @pl.when(t == TILES - 1)
        def _():
            sum_slices(part_ref, o_ref, SCALE)

    return by_tile(
        kernel,
        (rows, expand),
        jax.ShapeDtypeStruct((sources, SLOTS, 2 * rank), BF16),
        [pltpu.VMEM((sources, SLOTS, 2 * rank), F32)],
        2 * TILES * count * HELD * rank * width,
        whole_out=True,
    )


def spread_pairs(values, count, rank, t):
    held = values.reshape(count, 2 * rank).astype(F32)
    turned = pltpu.roll(held, rank, 1)
    first = iota((count, 2 * rank), 1) < rank
    halves = (jnp.where(first, held, turned), jnp.where(first, turned, held))
    block = row_block(count, t)
    return [
        jnp.concatenate(
            [jnp.where(pair_of(block, p), half, 0.0) for p in range(HELD // 2)], axis=1
        ).astype(BF16)
        for half in halves
    ]


def spread_blocks(values, count, rank, t):
    held = values.reshape(count, rank).astype(F32)
    block = row_block(count, t)
    return jnp.concatenate(
        [jnp.where(block == b, held, 0.0) for b in range(HELD)], axis=1
    ).astype(BF16)


def expand_rows(lowered, expand, split):
    sources = lowered.shape[0]
    count, rank, width = sources * TILE, expand.shape[1], expand.shape[2]

    def kernel(l_ref, w_ref, o_ref):
        t = pl.program_id(0)
        w = held_weights(w_ref, t)
        halves = spread_pairs(l_ref[...], count, rank, t)
        for half, lo, hi in zip(halves, (0, split), (split, width)):
            result = SCALE * jnp.dot(half, w[:, lo:hi], preferred_element_type=F32)
            o_ref[:, :, lo:hi] = result.astype(BF16).reshape(sources, TILE, hi - lo)

    return by_tile(
        kernel,
        (lowered, expand),
        jax.ShapeDtypeStruct((sources, SLOTS, width), BF16),
        [],
        2 * TILES * count * HELD * rank * width,
    )


def token_rows(backward, shrink):
    sources = backward.shape[0]
    count, rank, width = sources * TILE, shrink.shape[1], shrink.shape[2]

    def kernel(b_ref, w_ref, o_ref):
        t = pl.program_id(0)
        wide = spread_blocks(b_ref[...], count, rank, t)
        result = jnp.dot(wide, held_weights(w_ref, t), preferred_element_type=F32)
        o_ref[...] = result.astype(BF16).reshape(sources, TILE, width)

    return by_tile(
        kernel,
        (backward, shrink),
        jax.ShapeDtypeStruct((sources, SLOTS, width), BF16),
        [],
        2 * TILES * count * HELD * rank * width,
    )


def put_gradient(o_ref, carry_ref, pieces, rank, lo, hi):
    t = pl.program_id(0)
    first = pieces[:rank] + jnp.where(t > 0, carry_ref[:, lo:hi], 0.0)
    o_ref[STEP * t, :, lo:hi] = first.astype(BF16)
    inner = pieces[rank : STEP * rank].astype(BF16)
    o_ref[pl.ds(STEP * t + 1, STEP - 1), :, lo:hi] = inner.reshape(STEP - 1, rank, hi - lo)
    last = pieces[STEP * rank :]
    carry_ref[:, lo:hi] = last

    @pl.when(t == TILES - 1)
    def _():
        o_ref[BLOCKS - 1, :, lo:hi] = last.astype(BF16)


def expand_gradient(lowered, rows, rank, split):
    sources, _, width = rows.shape
    count = sources * TILE

    def kernel(l_ref, x_ref, o_ref, carry_ref):
        x = x_ref[...].reshape(count, width)
        halves = spread_pairs(l_ref[...], count, rank, pl.program_id(0))
        for half, lo, hi in zip(halves, (0, split), (split, width)):
            pieces = SCALE * lax.dot_general(
                half, x[:, lo:hi], (((0,), (0,)), ((), ())), preferred_element_type=F32
            )
            put_gradient(o_ref, carry_ref, pieces, rank, lo, hi)

    return by_tile(
        kernel,
        (lowered, rows),
        jax.ShapeDtypeStruct((BLOCKS, rank, width), BF16),
        [pltpu.VMEM((rank, width), F32)],
        2 * TILES * count * HELD * rank * width,
    )


def shrink_gradient(backward, rows):
    sources, _, width = rows.shape
    count, rank = sources * TILE, backward.shape[2]

    def kernel(b_ref, x_ref, o_ref, carry_ref):
        wide = spread_blocks(b_ref[...], count, rank, pl.program_id(0))
        pieces = lax.dot_general(
            wide,
            x_ref[...].reshape(count, width),
            (((0,), (0,)), ((), ())),
            preferred_element_type=F32,
        )
        put_gradient(o_ref, carry_ref, pieces, rank, 0, width)

    return by_tile(
        kernel,
        (backward, rows),
        jax.ShapeDtypeStruct((BLOCKS, rank, width), BF16),
        [pltpu.VMEM((rank, width), F32)],
        2 * TILES * count * HELD * rank * width,
    )


ROUTE = ("y", "c", "x")
PARTS = ("y", "c")
SWAP = ("y", "c", "z")


def exchange(values):
    return lax.all_to_all(values, ROUTE, 0, 0, tiled=True)


def swap(values):
    turns = [(j * CUTS + o, o * CUTS + j) for j in range(CUTS) for o in range(CUTS)]
    return lax.ppermute(values, SWAP, turns)


def gathered(shard):
    return lax.all_gather(swap(shard), "z", axis=0, tiled=True)


def summed(parts):
    return swap(lax.psum_scatter(parts, "z", scatter_dimension=0, tiled=True))


def body(tokens, adapter_index, query_cotangent, value_cotangent, shrink, query_expand, value_expand):
    sources = lax.axis_size(ROUTE)
    local, kinds, rank, width = shrink.shape
    value_width = value_expand.shape[2]

    sent_both = place(adapter_index, (query_cotangent, value_cotangent), sources)
    rows_both = exchange(sent_both)
    whole_expand = gathered(jnp.concatenate([query_expand, value_expand], axis=2))
    whole_shrink = gathered(shrink.reshape(local, kinds * rank, width))
    sent_tokens = place(adapter_index, (tokens,), sources)
    rows_tokens = exchange(sent_tokens)

    backward = backward_rows(rows_both, whole_expand, width)
    out_tokens = exchange(token_rows(backward, whole_shrink))
    grad_shrink = summed(shrink_gradient(backward, rows_tokens)).astype(F32)
    lowered = lowered_rows(rows_tokens, whole_shrink)
    out_both = exchange(expand_rows(lowered, whole_expand, width))
    grad_expand = summed(expand_gradient(lowered, rows_both, rank, width)).astype(F32)

    (token_gradient,) = collect(adapter_index, out_tokens, (width,))
    query_delta, value_delta = collect(adapter_index, out_both, (width, value_width))
    return (
        query_delta,
        value_delta,
        token_gradient,
        grad_shrink.reshape(local, kinds, rank, width),
        grad_expand[:, :, :width],
        grad_expand[:, :, width:],
    )


def solution(mesh):
    grid = Mesh(mesh.devices.reshape(4, 2, 4, 8), ("y", "c", "x", "z"))
    rows = P(("y", "c", "x", "z"), None)
    weights = (
        P(("x", "z"), None, None, PARTS),
        P(("x", "z"), None, PARTS),
        P(("x", "z"), None, PARTS),
    )

    return jax.shard_map(
        body,
        mesh=grid,
        in_specs=(rows, rows, rows, rows) + weights,
        out_specs=(rows, rows, rows) + weights,
        check_vma=False,
    )
```

```python
import jax
import jax.numpy as jnp
from jax import lax
from jax.experimental import pallas as pl
from jax.experimental.pallas import tpu as pltpu
from jax.sharding import Mesh, PartitionSpec as P


SCALE = 0.5
F32 = jnp.float32
BF16 = jnp.bfloat16
CAP = 3
PAIR = 2
CUTS = 8
BLOCKS = CUTS * PAIR
SLOTS = BLOCKS * CAP
EACH = PAIR * CAP
ROOM = 8
TILE = 16
TILES = SLOTS // TILE
STEP = 5
HELD = STEP + 1
NEAR = 4


def iota(shape, dim):
    return lax.broadcasted_iota(jnp.int32, shape, dim)


def whole_target(adapter, ordinal):
    dest = ((adapter >> 1) & 7) * 4 + (adapter >> 4)
    return dest * SLOTS + (adapter & 1) * CAP + ordinal


def cut_target(adapter, ordinal):
    return adapter * CAP + ordinal


def as_row(column):
    n = column.shape[0]
    return jnp.sum(jnp.where(iota((n, n), 0) == iota((n, n), 1), column, 0), axis=0, keepdims=True)


def target_row(adapter, target_of):
    n = adapter.shape[0]
    row = as_row(adapter)
    same = (adapter == row) & (iota((n, n), 0) < iota((n, n), 1))
    return target_of(row, jnp.sum(same.astype(jnp.int32), axis=0, keepdims=True))


def target_column(adapter, target_of):
    n = adapter.shape[0]
    same = (adapter == as_row(adapter)) & (iota((n, n), 1) < iota((n, n), 0))
    return target_of(adapter, jnp.sum(same.astype(jnp.int32), axis=1, keepdims=True))


def slot_at(index, t):
    return (index >> 4) * SLOTS + t * TILE + (index & (TILE - 1))


def row_block(rows, t):
    inner = (iota((rows, 128), 0) & (TILE - 1)) + t
    block = jnp.zeros((rows, 128), jnp.int32)
    for k in range(1, HELD):
        block = block + (inner >= CAP * k).astype(jnp.int32)
    return block


def pair_of(block, pair):
    half = (iota(block.shape, 1) >= 64).astype(jnp.int32)
    return block == 2 * pair + half


def params():
    return pltpu.CompilerParams(vmem_limit_bytes=30 << 20)


def cost(flops, moved):
    return pl.CostEstimate(flops=flops, bytes_accessed=moved, transcendentals=0)


def place(adapter, values, sources):
    n = adapter.shape[0]
    widths = [v.shape[1] // CUTS for v in values]
    total = sum(widths)
    count = sources * TILE

    def kernel(a_ref, *refs):
        ins, o_ref = refs[:-1], refs[-1]
        t = pl.program_id(0)
        first = target_row(a_ref[...], whole_target)
        slot = slot_at(iota((count, n), 0), t)
        spots = jnp.concatenate(
            [slot == first + PAIR * CAP * (2 * t + near) for near in range(NEAR)], axis=1
        )
        spots = spots.astype(F32).astype(BF16)
        at = 0
        for v_ref, width in zip(ins, widths):
            begin = pl.multiple_of(2 * t * width, 128)
            held = v_ref[:, pl.ds(begin, NEAR * width)]
            held = jnp.concatenate(
                [held[:, near * width : (near + 1) * width] for near in range(NEAR)], axis=0
            )
            moved = jnp.dot(spots, held, preferred_element_type=F32).astype(BF16)
            o_ref[:, :, at : at + width] = moved.reshape(sources, TILE, width)
            at += width

    return pl.pallas_call(
        kernel,
        grid=(TILES,),
        in_specs=[pl.BlockSpec((n, 1), lambda t: (0, 0))]
        + [pl.BlockSpec(v.shape, lambda t: (0, 0)) for v in values],
        out_specs=pl.BlockSpec((sources, TILE, total), lambda t: (0, t, 0)),
        out_shape=jax.ShapeDtypeStruct((sources, SLOTS, total), BF16),
        compiler_params=params(),
        cost_estimate=cost(2 * sources * SLOTS * n * NEAR * total, 2 * total * (CUTS * n + sources * SLOTS)),
    )(adapter, *values)


def collect(adapter, moved, widths):
    n = adapter.shape[0]
    sources, _, total = moved.shape
    count = sources * TILE

    def kernel(a_ref, m_ref, *outs):
        t = pl.program_id(0)
        first = target_column(a_ref[...], whole_target)
        slot = slot_at(iota((n, count), 1), t)
        spots = jnp.concatenate(
            [slot == first + PAIR * CAP * (2 * t + near) for near in range(NEAR)], axis=0
        )
        spots = spots.astype(F32).astype(BF16)
        at = 0
        for o_ref, width in zip(outs, widths):
            found = jnp.dot(
                spots, m_ref[:, :, at : at + width].reshape(count, width), preferred_element_type=F32
            )
            for near in range(NEAR):
                here = pl.ds(pl.multiple_of((2 * t + near) * width, 128), width)
                piece = found[near * n : (near + 1) * n]
                if near < 2:
                    piece = piece + jnp.where(t > 0, o_ref[:, here].astype(F32), 0.0)
                o_ref[:, here] = piece.astype(BF16)
            at += width

    return pl.pallas_call(
        kernel,
        grid=(TILES,),
        in_specs=[
            pl.BlockSpec((n, 1), lambda t: (0, 0)),
            pl.BlockSpec((sources, TILE, total), lambda t: (0, t, 0)),
        ],
        out_specs=[pl.BlockSpec((n, width * CUTS), lambda t: (0, 0)) for width in widths],
        out_shape=[jax.ShapeDtypeStruct((n, width * CUTS), BF16) for width in widths],
        compiler_params=params(),
        cost_estimate=cost(2 * sources * SLOTS * n * NEAR * total, 2 * total * (CUTS * n + sources * SLOTS)),
    )(adapter, moved)


def place_slices(adapter, values, sources):
    n, total = values.shape
    width = total // CUTS
    slots = sources // CUTS * SLOTS
    groups = sources // CUTS

    def kernel(a_ref, v_ref, o_ref, p_ref):
        @pl.when(pl.program_id(0) == 0)
        def _():
            spot = iota((slots, n), 0) == target_row(a_ref[...], cut_target)
            p_ref[...] = spot.astype(F32).astype(BF16)

        for k in range(2):
            moved = jnp.dot(
                p_ref[...], v_ref[:, k * width : (k + 1) * width], preferred_element_type=F32
            )
            o_ref[k * groups : (k + 1) * groups] = moved.astype(BF16).reshape(groups, SLOTS, width)

    return pl.pallas_call(
        kernel,
        grid=(CUTS // 2,),
        in_specs=[
            pl.BlockSpec((n, 1), lambda j: (0, 0)),
            pl.BlockSpec((n, 2 * width), lambda j: (0, j)),
        ],
        out_specs=pl.BlockSpec((2 * groups, SLOTS, width), lambda j: (j, 0, 0)),
        out_shape=jax.ShapeDtypeStruct((sources, SLOTS, width), BF16),
        scratch_shapes=[pltpu.VMEM((slots, n), BF16)],
        compiler_params=params(),
        cost_estimate=cost(2 * slots * n * total, 2 * total * (n + slots)),
    )(adapter, values)


def collect_slices(adapter, moved):
    n = adapter.shape[0]
    sources, _, width = moved.shape
    groups = sources // CUTS
    slots = groups * SLOTS

    def kernel(a_ref, m_ref, o_ref, p_ref):
        @pl.when(pl.program_id(0) == 0)
        def _():
            spot = iota((n, slots), 1) == target_column(a_ref[...], cut_target)
            p_ref[...] = spot.astype(F32).astype(BF16)

        for k in range(2):
            found = jnp.dot(
                p_ref[...],
                m_ref[k * groups : (k + 1) * groups].reshape(slots, width),
                preferred_element_type=F32,
            )
            o_ref[:, k * width : (k + 1) * width] = found.astype(BF16)

    return pl.pallas_call(
        kernel,
        grid=(CUTS // 2,),
        in_specs=[
            pl.BlockSpec((n, 1), lambda j: (0, 0)),
            pl.BlockSpec((2 * groups, SLOTS, width), lambda j: (j, 0, 0)),
        ],
        out_specs=pl.BlockSpec((n, 2 * width), lambda j: (0, j)),
        out_shape=jax.ShapeDtypeStruct((n, width * CUTS), BF16),
        scratch_shapes=[pltpu.VMEM((n, slots), BF16)],
        compiler_params=params(),
        cost_estimate=cost(2 * slots * n * width * CUTS, 2 * width * CUTS * (n + slots)),
    )(adapter, moved)


def held_weights(w_ref, t):
    _, rank, width = w_ref.shape
    return w_ref[pl.ds(STEP * t, HELD)].reshape(HELD * rank, width)


def by_tile(kernel, ins, out, scratch, flops, whole_out=False):
    def spec(shape):
        if shape[1] == SLOTS:
            return pl.BlockSpec((shape[0], TILE, shape[2]), lambda t: (0, t, 0))
        return pl.BlockSpec(shape, lambda t: (0, 0, 0))

    moved = sum(v.size * v.dtype.itemsize for v in ins) + out.size * out.dtype.itemsize
    return pl.pallas_call(
        kernel,
        grid=(TILES,),
        in_specs=[spec(v.shape) for v in ins],
        out_specs=pl.BlockSpec(out.shape, lambda t: (0,) * len(out.shape)) if whole_out else spec(out.shape),
        out_shape=out,
        scratch_shapes=scratch,
        compiler_params=params(),
        cost_estimate=cost(flops, moved),
    )(*ins)


def total_of_slices(part_ref):
    half = SLOTS // 2
    total = part_ref[:, :half, :] + part_ref[:, half:, :]
    total = total + pltpu.roll(total, half // 2, 1)
    total = total + pltpu.roll(total, half // 4, 1)
    return total


def keep_part(part_ref, t, part):
    for tile in range(TILES):

        @pl.when(t == tile)
        def _(tile=tile):
            part_ref[:, tile * TILE : (tile + 1) * TILE, :] = part


def lowered_part(rows, shrink):
    sources, _, width = rows.shape
    count, rank = sources * TILE, shrink.shape[1]

    def kernel(x_ref, w_ref, o_ref, part_ref):
        t = pl.program_id(0)
        dense = lax.dot_general(
            x_ref[...].reshape(count, width),
            held_weights(w_ref, t),
            (((1,), (1,)), ((), ())),
            preferred_element_type=F32,
        )
        block = row_block(count, t)
        total = jnp.zeros((count, rank), F32)
        for b in range(HELD):
            total = total + jnp.where(block == b, dense[:, b * rank : (b + 1) * rank], 0.0)
        keep_part(part_ref, t, total.reshape(sources, TILE, rank))

        @pl.when(t == TILES - 1)
        def _():
            o_ref[...] = jnp.zeros_like(o_ref)
            for p in range(CUTS):
                o_ref[p, :, :EACH, :] = part_ref[:, EACH * p : EACH * (p + 1), :]

    out = jax.ShapeDtypeStruct((CUTS, sources, ROOM, rank), F32)
    return by_tile(
        kernel,
        (rows, shrink),
        out,
        [pltpu.VMEM((sources, SLOTS, rank), F32)],
        2 * TILES * count * HELD * rank * width,
        whole_out=True,
    )


def lowered_sum(parts):
    _, sources, _, rank = parts.shape

    def kernel(p_ref, o_ref, held_ref):
        total = p_ref[0]
        for p in range(1, CUTS):
            total = total + p_ref[p]
        for k in range(CUTS):
            held_ref[:, EACH * k : EACH * (k + 1), :] = total[:, :EACH, :]
        o_ref[...] = held_ref[...].astype(BF16)

    return pl.pallas_call(
        kernel,
        out_shape=jax.ShapeDtypeStruct((sources, SLOTS, rank), BF16),
        scratch_shapes=[pltpu.VMEM((sources, SLOTS, rank), F32)],
        compiler_params=params(),
        cost_estimate=cost(parts.size, 4 * parts.size),
        name="lowered_sum",
    )(parts)


def backward_join(owned, sources):
    rank = owned.shape[1]

    def kernel(b_ref, o_ref, held_ref):
        owned_rows = b_ref[...].astype(F32).reshape(CUTS, sources, ROOM, rank)
        for p in range(CUTS):
            held_ref[:, EACH * p : EACH * (p + 1), :] = owned_rows[p][:, :EACH, :]
        o_ref[...] = held_ref[...].astype(BF16)

    return pl.pallas_call(
        kernel,
        out_shape=jax.ShapeDtypeStruct((sources, SLOTS, rank), BF16),
        scratch_shapes=[pltpu.VMEM((sources, SLOTS, rank), F32)],
        compiler_params=params(),
        cost_estimate=cost(owned.size, 4 * owned.size),
        name="backward_join",
    )(owned)


def backward_rows(rows, expand, split):
    sources, _, width = rows.shape
    count, rank = sources * TILE, expand.shape[1]

    def kernel(x_ref, w_ref, o_ref, part_ref):
        t = pl.program_id(0)
        x = x_ref[...].reshape(count, width)
        w = held_weights(w_ref, t)
        block = row_block(count, t)

        def part(lo, hi):
            dense = lax.dot_general(
                x[:, lo:hi], w[:, lo:hi], (((1,), (1,)), ((), ())), preferred_element_type=F32
            )
            total = jnp.zeros((count, 2 * rank), F32)
            for p in range(HELD // 2):
                piece = dense[:, 2 * rank * p : 2 * rank * (p + 1)]
                total = total + jnp.where(pair_of(block, p), piece, 0.0)
            return total + pltpu.roll(total, rank, 1)

        first = iota((count, 2 * rank), 1) < rank
        both = jnp.where(first, part(0, split), part(split, width))
        keep_part(part_ref, t, both.reshape(sources, TILE, 2 * rank))

        @pl.when(t == TILES - 1)
        def _():
            total = SCALE * total_of_slices(part_ref)[:, :ROOM, :]
            o_ref[...] = total.reshape(1, sources * ROOM, 2 * rank).astype(BF16)

    return by_tile(
        kernel,
        (rows, expand),
        jax.ShapeDtypeStruct((1, sources * ROOM, 2 * rank), BF16),
        [pltpu.VMEM((sources, SLOTS, 2 * rank), F32)],
        2 * TILES * count * HELD * rank * width,
        whole_out=True,
    )


def spread_pairs(values, count, rank, t):
    held = values.reshape(count, 2 * rank).astype(F32)
    turned = pltpu.roll(held, rank, 1)
    first = iota((count, 2 * rank), 1) < rank
    halves = (jnp.where(first, held, turned), jnp.where(first, turned, held))
    block = row_block(count, t)
    return [
        jnp.concatenate(
            [jnp.where(pair_of(block, p), half, 0.0) for p in range(HELD // 2)], axis=1
        ).astype(BF16)
        for half in halves
    ]


def spread_blocks(values, count, rank, t):
    held = values.reshape(count, rank).astype(F32)
    block = row_block(count, t)
    return jnp.concatenate(
        [jnp.where(block == b, held, 0.0) for b in range(HELD)], axis=1
    ).astype(BF16)


def expand_rows(lowered, expand, split):
    sources = lowered.shape[0]
    count, rank, width = sources * TILE, expand.shape[1], expand.shape[2]

    def kernel(l_ref, w_ref, o_ref):
        t = pl.program_id(0)
        w = held_weights(w_ref, t)
        halves = spread_pairs(l_ref[...], count, rank, t)
        for half, lo, hi in zip(halves, (0, split), (split, width)):
            result = SCALE * jnp.dot(half, w[:, lo:hi], preferred_element_type=F32)
            o_ref[:, :, lo:hi] = result.astype(BF16).reshape(sources, TILE, hi - lo)

    return by_tile(
        kernel,
        (lowered, expand),
        jax.ShapeDtypeStruct((sources, SLOTS, width), BF16),
        [],
        2 * TILES * count * HELD * rank * width,
    )


def token_rows(backward, shrink):
    sources = backward.shape[0]
    count, rank, width = sources * TILE, shrink.shape[1], shrink.shape[2]

    def kernel(b_ref, w_ref, o_ref):
        t = pl.program_id(0)
        wide = spread_blocks(b_ref[...], count, rank, t)
        result = jnp.dot(wide, held_weights(w_ref, t), preferred_element_type=F32)
        o_ref[...] = result.astype(BF16).reshape(sources, TILE, width)

    return by_tile(
        kernel,
        (backward, shrink),
        jax.ShapeDtypeStruct((sources, SLOTS, width), BF16),
        [],
        2 * TILES * count * HELD * rank * width,
    )


def put_gradient(o_ref, carry_ref, pieces, rank, lo, hi):
    t = pl.program_id(0)
    first = pieces[:rank] + jnp.where(t > 0, carry_ref[:, lo:hi], 0.0)
    o_ref[STEP * t, :, lo:hi] = first.astype(BF16)
    inner = pieces[rank : STEP * rank].astype(BF16)
    o_ref[pl.ds(STEP * t + 1, STEP - 1), :, lo:hi] = inner.reshape(STEP - 1, rank, hi - lo)
    last = pieces[STEP * rank :]
    carry_ref[:, lo:hi] = last

    @pl.when(t == TILES - 1)
    def _():
        o_ref[BLOCKS - 1, :, lo:hi] = last.astype(BF16)


def expand_gradient(lowered, rows, rank, split):
    sources, _, width = rows.shape
    count = sources * TILE

    def kernel(l_ref, x_ref, o_ref, carry_ref):
        x = x_ref[...].reshape(count, width)
        halves = spread_pairs(l_ref[...], count, rank, pl.program_id(0))
        for half, lo, hi in zip(halves, (0, split), (split, width)):
            pieces = SCALE * lax.dot_general(
                half, x[:, lo:hi], (((0,), (0,)), ((), ())), preferred_element_type=F32
            )
            put_gradient(o_ref, carry_ref, pieces, rank, lo, hi)

    return by_tile(
        kernel,
        (lowered, rows),
        jax.ShapeDtypeStruct((BLOCKS, rank, width), BF16),
        [pltpu.VMEM((rank, width), F32)],
        2 * TILES * count * HELD * rank * width,
    )


def shrink_gradient(backward, rows):
    sources, _, width = rows.shape
    count, rank = sources * TILE, backward.shape[2]

    def kernel(b_ref, x_ref, o_ref, carry_ref):
        wide = spread_blocks(b_ref[...], count, rank, pl.program_id(0))
        pieces = lax.dot_general(
            wide,
            x_ref[...].reshape(count, width),
            (((0,), (0,)), ((), ())),
            preferred_element_type=F32,
        )
        put_gradient(o_ref, carry_ref, pieces, rank, 0, width)

    return by_tile(
        kernel,
        (backward, rows),
        jax.ShapeDtypeStruct((BLOCKS, rank, width), BF16),
        [pltpu.VMEM((rank, width), F32)],
        2 * TILES * count * HELD * rank * width,
    )


ROUTE = ("y", "c", "x")
PARTS = ("y", "c")
SWAP = ("y", "c", "z")


def exchange(values):
    return lax.all_to_all(values, ROUTE, 0, 0, tiled=True)


def swap(values):
    turns = [(j * CUTS + o, o * CUTS + j) for j in range(CUTS) for o in range(CUTS)]
    return lax.ppermute(values, SWAP, turns)


def gathered(shard):
    return lax.all_gather(shard, "z", axis=0, tiled=True)


def summed(parts):
    return lax.psum_scatter(parts, "z", scatter_dimension=0, tiled=True)


def body(tokens, adapter_index, query_cotangent, value_cotangent, shrink, query_expand, value_expand):
    sources = lax.axis_size(ROUTE)
    local, kinds, rank, width = shrink.shape
    value_width = value_expand.shape[2]

    whole_shrink = gathered(shrink.reshape(local, kinds * rank, width))
    sent_tokens = place_slices(adapter_index, tokens, sources)
    rows_tokens = exchange(sent_tokens)
    own_expand = swap(jnp.concatenate([query_expand, value_expand], axis=2))
    whole_expand = gathered(own_expand)
    sent_both = place(adapter_index, (query_cotangent, value_cotangent), sources)
    rows_both = exchange(sent_both)

    part = lowered_part(rows_tokens, whole_shrink)
    parts = lax.all_to_all(part, PARTS, 0, 0, tiled=True)
    lowered = lowered_sum(parts)
    owned = backward_rows(rows_both, whole_expand, width)[0]
    owned = lax.all_gather(owned, PARTS, axis=0, tiled=True)
    backward = backward_join(owned, sources)

    out_both = exchange(expand_rows(lowered, whole_expand, width))
    grad_expand = summed(expand_gradient(lowered, rows_both, rank, width))
    grad_expand = swap(grad_expand).astype(F32)
    out_tokens = exchange(token_rows(backward, whole_shrink))
    grad_shrink = summed(shrink_gradient(backward, rows_tokens)).astype(F32)

    query_delta, value_delta = collect(adapter_index, out_both, (width, value_width))
    token_gradient = collect_slices(adapter_index, out_tokens)
    return (
        query_delta,
        value_delta,
        token_gradient,
        grad_shrink.reshape(local, kinds, rank, width),
        grad_expand[:, :, :width],
        grad_expand[:, :, width:],
    )


def solution(mesh):
    grid = Mesh(mesh.devices.reshape(4, 2, 4, 8), ("y", "c", "x", "z"))
    rows = P(("y", "c", "x", "z"), None)
    weights = (
        P(("x", "z"), None, None, PARTS),
        P(("x", "z"), None, PARTS),
        P(("x", "z"), None, PARTS),
    )

    return jax.shard_map(
        body,
        mesh=grid,
        in_specs=(rows, rows, rows, rows) + weights,
        out_specs=(rows, rows, rows) + weights,
        check_vma=False,
    )
```

```python
import jax
import jax.numpy as jnp
from jax import lax
from jax.experimental import pallas as pl
from jax.experimental.pallas import tpu as pltpu
from jax.sharding import Mesh, PartitionSpec as P


SCALE = 0.5
F32 = jnp.float32
BF16 = jnp.bfloat16
CAP = 3
CUTS = 8
BLOCKS = 16
SLOTS = BLOCKS * CAP
TILE = 16
TILES = SLOTS // TILE
STEP = 5
HELD = STEP + 1


def iota(shape, dim):
    return lax.broadcasted_iota(jnp.int32, shape, dim)


def cut_target(adapter, ordinal):
    return adapter * CAP + ordinal


def as_row(column):
    n = column.shape[0]
    return jnp.sum(jnp.where(iota((n, n), 0) == iota((n, n), 1), column, 0), axis=0, keepdims=True)


def target_row(adapter):
    n = adapter.shape[0]
    row = as_row(adapter)
    same = (adapter == row) & (iota((n, n), 0) < iota((n, n), 1))
    return cut_target(row, jnp.sum(same.astype(jnp.int32), axis=0, keepdims=True))


def target_column(adapter):
    n = adapter.shape[0]
    same = (adapter == as_row(adapter)) & (iota((n, n), 1) < iota((n, n), 0))
    return cut_target(adapter, jnp.sum(same.astype(jnp.int32), axis=1, keepdims=True))


def row_block(rows, t):
    inner = (iota((rows, 128), 0) & (TILE - 1)) + t
    block = jnp.zeros((rows, 128), jnp.int32)
    for k in range(1, HELD):
        block = block + (inner >= CAP * k).astype(jnp.int32)
    return block


def pair_of(block, pair):
    half = (iota(block.shape, 1) >= 64).astype(jnp.int32)
    return block == 2 * pair + half


def params():
    return pltpu.CompilerParams(vmem_limit_bytes=40 << 20)


def cost(flops, moved):
    return pl.CostEstimate(flops=flops, bytes_accessed=moved, transcendentals=0)


def place(adapter, values, sources):
    n = adapter.shape[0]
    widths = [v.shape[1] // CUTS for v in values]
    total = sum(widths)
    groups = sources // CUTS
    slots = groups * SLOTS

    def kernel(a_ref, *refs):
        ins, o_ref, p_ref = refs[:-2], refs[-2], refs[-1]

        @pl.when(pl.program_id(0) == 0)
        def _():
            spot = iota((slots, n), 0) == target_row(a_ref[...])
            p_ref[...] = spot.astype(F32).astype(BF16)

        at = 0
        for v_ref, width in zip(ins, widths):
            for k in range(2):
                moved = jnp.dot(
                    p_ref[...], v_ref[:, k * width : (k + 1) * width], preferred_element_type=F32
                )
                moved = moved.astype(BF16).reshape(groups, SLOTS, width)
                o_ref[k * groups : (k + 1) * groups, :, at : at + width] = moved
            at += width

    return pl.pallas_call(
        kernel,
        grid=(CUTS // 2,),
        in_specs=[pl.BlockSpec((n, 1), lambda j: (0, 0))]
        + [pl.BlockSpec((n, 2 * width), lambda j: (0, j)) for width in widths],
        out_specs=pl.BlockSpec((2 * groups, SLOTS, total), lambda j: (j, 0, 0)),
        out_shape=jax.ShapeDtypeStruct((sources, SLOTS, total), BF16),
        scratch_shapes=[pltpu.VMEM((slots, n), BF16)],
        compiler_params=params(),
        cost_estimate=cost(2 * slots * n * total * CUTS, 2 * total * CUTS * (n + slots)),
    )(adapter, *values)


def collect(adapter, moved, widths):
    n = adapter.shape[0]
    sources, _, total = moved.shape
    groups = sources // CUTS
    slots = groups * SLOTS

    def kernel(a_ref, m_ref, *refs):
        outs, p_ref = refs[:-1], refs[-1]

        @pl.when(pl.program_id(0) == 0)
        def _():
            spot = iota((n, slots), 1) == target_column(a_ref[...])
            p_ref[...] = spot.astype(F32).astype(BF16)

        at = 0
        for o_ref, width in zip(outs, widths):
            for k in range(2):
                found = jnp.dot(
                    p_ref[...],
                    m_ref[k * groups : (k + 1) * groups, :, at : at + width].reshape(slots, width),
                    preferred_element_type=F32,
                )
                o_ref[:, k * width : (k + 1) * width] = found.astype(BF16)
            at += width

    return pl.pallas_call(
        kernel,
        grid=(CUTS // 2,),
        in_specs=[
            pl.BlockSpec((n, 1), lambda j: (0, 0)),
            pl.BlockSpec((2 * groups, SLOTS, total), lambda j: (j, 0, 0)),
        ],
        out_specs=[pl.BlockSpec((n, 2 * width), lambda j: (0, j)) for width in widths],
        out_shape=[jax.ShapeDtypeStruct((n, width * CUTS), BF16) for width in widths],
        scratch_shapes=[pltpu.VMEM((n, slots), BF16)],
        compiler_params=params(),
        cost_estimate=cost(2 * slots * n * total * CUTS, 2 * total * CUTS * (n + slots)),
    )(adapter, moved)


def held_weights(w_ref, t):
    _, rank, width = w_ref.shape
    return w_ref[pl.ds(STEP * t, HELD)].reshape(HELD * rank, width)


def by_tile(kernel, ins, out, scratch, flops, whole_out=False):
    def spec(shape):
        if shape[1] == SLOTS:
            return pl.BlockSpec((shape[0], TILE, shape[2]), lambda t: (0, t, 0))
        return pl.BlockSpec(shape, lambda t: (0, 0, 0))

    moved = sum(v.size * v.dtype.itemsize for v in ins) + out.size * out.dtype.itemsize
    return pl.pallas_call(
        kernel,
        grid=(TILES,),
        in_specs=[spec(v.shape) for v in ins],
        out_specs=pl.BlockSpec(out.shape, lambda t: (0,) * len(out.shape)) if whole_out else spec(out.shape),
        out_shape=out,
        scratch_shapes=scratch,
        compiler_params=params(),
        cost_estimate=cost(flops, moved),
    )(*ins)


def lowered_part(rows, shrink):
    sources, _, width = rows.shape
    count, rank = sources * TILE, shrink.shape[1]

    def kernel(x_ref, w_ref, o_ref):
        t = pl.program_id(0)
        dense = lax.dot_general(
            x_ref[...].reshape(count, width),
            held_weights(w_ref, t),
            (((1,), (1,)), ((), ())),
            preferred_element_type=F32,
        )
        block = row_block(count, t)
        total = jnp.zeros((count, rank), F32)
        for b in range(HELD):
            total = total + jnp.where(block == b, dense[:, b * rank : (b + 1) * rank], 0.0)
        o_ref[...] = total.reshape(sources, TILE, rank)

    return by_tile(
        kernel,
        (rows, shrink),
        jax.ShapeDtypeStruct((sources, SLOTS, rank), F32),
        [],
        2 * TILES * count * HELD * rank * width,
    )


def backward_part(rows, expand, split):
    sources, _, width = rows.shape
    count, rank = sources * TILE, expand.shape[1]

    def kernel(x_ref, w_ref, o_ref):
        t = pl.program_id(0)
        x = x_ref[...].reshape(count, width)
        w = held_weights(w_ref, t)
        block = row_block(count, t)

        def part(lo, hi):
            dense = lax.dot_general(
                x[:, lo:hi], w[:, lo:hi], (((1,), (1,)), ((), ())), preferred_element_type=F32
            )
            total = jnp.zeros((count, 2 * rank), F32)
            for p in range(HELD // 2):
                piece = dense[:, 2 * rank * p : 2 * rank * (p + 1)]
                total = total + jnp.where(pair_of(block, p), piece, 0.0)
            return total + pltpu.roll(total, rank, 1)

        first = iota((count, 2 * rank), 1) < rank
        both = jnp.where(first, part(0, split), part(split, width))
        o_ref[...] = both.reshape(sources, TILE, 2 * rank)

    return by_tile(
        kernel,
        (rows, expand),
        jax.ShapeDtypeStruct((sources, SLOTS, 2 * rank), F32),
        [],
        2 * TILES * count * HELD * rank * width,
    )


def join_sums(low, back):
    parts, count, rank = low.shape

    def kernel(l_ref, b_ref, o_ref):
        for ref, factor, at in ((l_ref, 1.0, 0), (b_ref, SCALE, rank)):
            total = ref[0]
            for p in range(1, parts):
                total = total + ref[p]
            o_ref[:, at : at + rank] = (factor * total).astype(BF16)

    return pl.pallas_call(
        kernel,
        out_shape=jax.ShapeDtypeStruct((count, 2 * rank), BF16),
        compiler_params=params(),
        cost_estimate=cost(2 * low.size, 8 * low.size),
        name="join_sums",
    )(low, back)


def spread_pairs(values, count, rank, t):
    held = values.reshape(count, 2 * rank).astype(F32)
    turned = pltpu.roll(held, rank, 1)
    first = iota((count, 2 * rank), 1) < rank
    halves = (jnp.where(first, held, turned), jnp.where(first, turned, held))
    block = row_block(count, t)
    return [
        jnp.concatenate(
            [jnp.where(pair_of(block, p), half, 0.0) for p in range(HELD // 2)], axis=1
        ).astype(BF16)
        for half in halves
    ]


def spread_blocks(values, count, rank, t):
    held = values.reshape(count, rank).astype(F32)
    block = row_block(count, t)
    return jnp.concatenate(
        [jnp.where(block == b, held, 0.0) for b in range(HELD)], axis=1
    ).astype(BF16)


def expand_rows(joint, expand, split):
    sources = joint.shape[0]
    count, rank, width = sources * TILE, expand.shape[1], expand.shape[2]

    def kernel(l_ref, w_ref, o_ref):
        t = pl.program_id(0)
        w = held_weights(w_ref, t)
        halves = spread_pairs(l_ref[:, :, : 2 * rank], count, rank, t)
        for half, lo, hi in zip(halves, (0, split), (split, width)):
            result = SCALE * jnp.dot(half, w[:, lo:hi], preferred_element_type=F32)
            o_ref[:, :, lo:hi] = result.astype(BF16).reshape(sources, TILE, hi - lo)

    return by_tile(
        kernel,
        (joint, expand),
        jax.ShapeDtypeStruct((sources, SLOTS, width), BF16),
        [],
        2 * TILES * count * HELD * rank * width,
    )


def token_rows(joint, shrink):
    sources = joint.shape[0]
    count, rank, width = sources * TILE, shrink.shape[1], shrink.shape[2]

    def kernel(b_ref, w_ref, o_ref):
        t = pl.program_id(0)
        wide = spread_blocks(b_ref[:, :, rank:], count, rank, t)
        result = jnp.dot(wide, held_weights(w_ref, t), preferred_element_type=F32)
        o_ref[...] = result.astype(BF16).reshape(sources, TILE, width)

    return by_tile(
        kernel,
        (joint, shrink),
        jax.ShapeDtypeStruct((sources, SLOTS, width), BF16),
        [],
        2 * TILES * count * HELD * rank * width,
    )


def add_carry(carry_ref, pieces, rank, lo, hi):
    t = pl.program_id(0)
    first = pieces[:rank] + jnp.where(t > 0, carry_ref[:, lo:hi], 0.0)
    carry_ref[:, lo:hi] = pieces[STEP * rank :]
    done = jnp.concatenate([first, pieces[rank : STEP * rank]], axis=0)
    return done.astype(BF16).reshape(STEP, rank, hi - lo)


def fold(piece, width):
    narrow = piece.shape[-1]
    return jnp.concatenate([piece[..., 8 * i : 8 * i + 8, :] for i in range(width // narrow)], axis=-1)


def gradients(joint, rows_tokens, rows_both, split):
    sources, _, both = rows_both.shape
    count, pair = sources * TILE, joint.shape[2] // 2
    rank = pair // 2
    height = pair + rank + 8

    def put(o_ref, at, size, begin, end, value):
        o_ref[pl.ds(at, size), begin:end, :] = value

    def kernel(j_ref, t_ref, x_ref, o_ref, shrink_ref, expand_ref):
        t = pl.program_id(0)
        turn = (((0,), (0,)), ((), ()))
        wide = spread_blocks(j_ref[:, :, pair:], count, pair, t)
        tokens = t_ref[...].reshape(count, split)
        pieces = lax.dot_general(wide, tokens, turn, preferred_element_type=F32)
        put(o_ref, STEP * t, STEP, 0, pair, add_carry(shrink_ref, pieces, pair, 0, split))

        x = x_ref[...].reshape(count, both)
        halves = spread_pairs(j_ref[:, :, :pair], count, rank, t)
        pieces = SCALE * lax.dot_general(halves[0], x[:, :split], turn, preferred_element_type=F32)
        put(o_ref, STEP * t, STEP, pair, pair + rank, add_carry(expand_ref, pieces, rank, 0, split))
        pieces = SCALE * lax.dot_general(halves[1], x[:, split:], turn, preferred_element_type=F32)
        first = pieces[:rank] + jnp.where(t > 0, expand_ref[:, split:], 0.0)
        expand_ref[:, split:] = pieces[STEP * rank :]
        for b in range(STEP):
            piece = first if b == 0 else pieces[b * rank : (b + 1) * rank]
            o_ref[STEP * t + b, pair + rank :, :] = fold(piece, split).astype(BF16)

        @pl.when(t == TILES - 1)
        def _():
            o_ref[BLOCKS - 1, :pair, :] = shrink_ref[...].astype(BF16)
            o_ref[BLOCKS - 1, pair : pair + rank, :] = expand_ref[:, :split].astype(BF16)
            o_ref[BLOCKS - 1, pair + rank :, :] = fold(expand_ref[:, split:], split).astype(BF16)

    return by_tile(
        kernel,
        (joint, rows_tokens, rows_both),
        jax.ShapeDtypeStruct((BLOCKS, height, split), BF16),
        [pltpu.VMEM((pair, split), F32), pltpu.VMEM((rank, both), F32)],
        2 * TILES * count * HELD * (pair * split + rank * both),
        whole_out=True,
    )


def unpack(sums, rank, narrow):
    local, _, width = sums.shape
    pair = 2 * rank

    def kernel(g_ref, s_ref, q_ref, v_ref):
        s_ref[...] = g_ref[:, :pair, :].astype(F32)
        q_ref[...] = g_ref[:, pair : pair + rank, :].astype(F32)
        last = g_ref[:, pair + rank :, :].astype(F32)
        for i in range(width // narrow):
            v_ref[:, 8 * i : 8 * i + 8, :] = last[:, :, narrow * i : narrow * (i + 1)]

    return pl.pallas_call(
        kernel,
        out_shape=[
            jax.ShapeDtypeStruct((local, pair, width), F32),
            jax.ShapeDtypeStruct((local, rank, width), F32),
            jax.ShapeDtypeStruct((local, rank, narrow), F32),
        ],
        compiler_params=params(),
        cost_estimate=cost(sums.size, 6 * sums.size),
        name="unpack",
    )(sums)


ROUTE = ("y", "c", "x")
PARTS = ("y", "c")


def exchange(values):
    return lax.all_to_all(values, ROUTE, 0, 0, tiled=True)


def gathered(shard):
    return lax.all_gather(shard, "z", axis=0, tiled=True)


def summed(parts):
    return lax.psum_scatter(parts, "z", scatter_dimension=0, tiled=True)


def small_exchange(part):
    parts = lax.axis_size(PARTS)
    sources, slots, rank = part.shape
    return lax.all_to_all(part.reshape(parts, sources * slots // parts, rank), PARTS, 0, 0, tiled=True)


def body(tokens, adapter_index, query_cotangent, value_cotangent, shrink, query_expand, value_expand):
    sources = lax.axis_size(ROUTE)
    local, kinds, rank, width = shrink.shape
    value_width = value_expand.shape[2]

    whole_shrink = gathered(shrink.reshape(local, kinds * rank, width))
    sent_tokens = place(adapter_index, (tokens,), sources)
    rows_tokens = exchange(sent_tokens)
    whole_expand = gathered(jnp.concatenate([query_expand, value_expand], axis=2))
    sent_both = place(adapter_index, (query_cotangent, value_cotangent), sources)
    rows_both = exchange(sent_both)

    low = small_exchange(lowered_part(rows_tokens, whole_shrink))
    back = small_exchange(backward_part(rows_both, whole_expand, width))
    joint = lax.all_gather(join_sums(low, back), PARTS, axis=0, tiled=True)
    joint = joint.reshape(sources, SLOTS, 4 * rank)

    out_both = exchange(expand_rows(joint, whole_expand, width))
    sums = summed(gradients(joint, rows_tokens, rows_both, width))
    out_tokens = exchange(token_rows(joint, whole_shrink))

    query_delta, value_delta = collect(adapter_index, out_both, (width, value_width))
    (token_gradient,) = collect(adapter_index, out_tokens, (width,))
    grad_shrink, grad_query, grad_value = unpack(sums, rank, value_width)
    return (
        query_delta,
        value_delta,
        token_gradient,
        grad_shrink.reshape(local, kinds, rank, width),
        grad_query,
        grad_value,
    )


def solution(mesh):
    grid = Mesh(mesh.devices.reshape(4, 2, 4, 8), ("y", "c", "x", "z"))
    rows = P(("y", "c", "x", "z"), None)
    weights = (
        P(("x", "z"), None, None, PARTS),
        P(("x", "z"), None, PARTS),
        P(("x", "z"), None, PARTS),
    )

    return jax.shard_map(
        body,
        mesh=grid,
        in_specs=(rows, rows, rows, rows) + weights,
        out_specs=(rows, rows, rows) + weights,
        check_vma=False,
    )
```

```python
import jax
import jax.numpy as jnp
from jax import lax
from jax.experimental import pallas as pl
from jax.experimental.pallas import tpu as pltpu
from jax.sharding import Mesh, PartitionSpec as P


SCALE = 0.5
F32 = jnp.float32
BF16 = jnp.bfloat16
CAP = 3
CUTS = 8
BLOCKS = 16
SLOTS = BLOCKS * CAP
TILE = 16
TILES = SLOTS // TILE
STEP = 5
HELD = STEP + 1


def iota(shape, dim):
    return lax.broadcasted_iota(jnp.int32, shape, dim)


def cut_target(adapter, ordinal):
    return adapter * CAP + ordinal


def as_row(column):
    n = column.shape[0]
    return jnp.sum(jnp.where(iota((n, n), 0) == iota((n, n), 1), column, 0), axis=0, keepdims=True)


def target_row(adapter):
    n = adapter.shape[0]
    row = as_row(adapter)
    same = (adapter == row) & (iota((n, n), 0) < iota((n, n), 1))
    return cut_target(row, jnp.sum(same.astype(jnp.int32), axis=0, keepdims=True))


def target_column(adapter):
    n = adapter.shape[0]
    same = (adapter == as_row(adapter)) & (iota((n, n), 1) < iota((n, n), 0))
    return cut_target(adapter, jnp.sum(same.astype(jnp.int32), axis=1, keepdims=True))


def row_block(rows, t):
    inner = (iota((rows, 128), 0) & (TILE - 1)) + t
    block = jnp.zeros((rows, 128), jnp.int32)
    for k in range(1, HELD):
        block = block + (inner >= CAP * k).astype(jnp.int32)
    return block


def pair_of(block, pair):
    half = (iota(block.shape, 1) >= 64).astype(jnp.int32)
    return block == 2 * pair + half


def params():
    return pltpu.CompilerParams(vmem_limit_bytes=40 << 20)


def cost(flops, moved):
    return pl.CostEstimate(flops=flops, bytes_accessed=moved, transcendentals=0)


def place(adapter, values, sources):
    n = adapter.shape[0]
    widths = [v.shape[1] // CUTS for v in values]
    total = sum(widths)
    groups = sources // CUTS
    slots = groups * SLOTS

    def kernel(a_ref, *refs):
        ins, o_ref, p_ref = refs[:-2], refs[-2], refs[-1]

        @pl.when(pl.program_id(0) == 0)
        def _():
            spot = iota((slots, n), 0) == target_row(a_ref[...])
            p_ref[...] = spot.astype(F32).astype(BF16)

        at = 0
        for v_ref, width in zip(ins, widths):
            for k in range(2):
                moved = jnp.dot(
                    p_ref[...], v_ref[:, k * width : (k + 1) * width], preferred_element_type=F32
                )
                moved = moved.astype(BF16).reshape(groups, SLOTS, width)
                o_ref[k * groups : (k + 1) * groups, :, at : at + width] = moved
            at += width

    return pl.pallas_call(
        kernel,
        grid=(CUTS // 2,),
        in_specs=[pl.BlockSpec((n, 1), lambda j: (0, 0))]
        + [pl.BlockSpec((n, 2 * width), lambda j: (0, j)) for width in widths],
        out_specs=pl.BlockSpec((2 * groups, SLOTS, total), lambda j: (j, 0, 0)),
        out_shape=jax.ShapeDtypeStruct((sources, SLOTS, total), BF16),
        scratch_shapes=[pltpu.VMEM((slots, n), BF16)],
        compiler_params=params(),
        cost_estimate=cost(2 * slots * n * total * CUTS, 2 * total * CUTS * (n + slots)),
    )(adapter, *values)


def find_slots(adapter, slots):
    n = adapter.shape[0]

    def kernel(a_ref, o_ref):
        spot = iota((n, slots), 1) == target_column(a_ref[...])
        o_ref[...] = spot.astype(F32).astype(BF16)

    return pl.pallas_call(
        kernel,
        out_shape=jax.ShapeDtypeStruct((n, slots), BF16),
        compiler_params=params(),
        cost_estimate=cost(n * slots, 2 * n * slots),
        name="find_slots",
    )(adapter)


def collect(spots, moved, widths):
    n, slots = spots.shape
    sources, _, total = moved.shape
    groups = sources // CUTS

    def kernel(p_ref, m_ref, *outs):
        at = 0
        for o_ref, width in zip(outs, widths):
            for k in range(2):
                found = jnp.dot(
                    p_ref[...],
                    m_ref[k * groups : (k + 1) * groups, :, at : at + width].reshape(slots, width),
                    preferred_element_type=F32,
                )
                o_ref[:, k * width : (k + 1) * width] = found.astype(BF16)
            at += width

    return pl.pallas_call(
        kernel,
        grid=(CUTS // 2,),
        in_specs=[
            pl.BlockSpec((n, slots), lambda j: (0, 0)),
            pl.BlockSpec((2 * groups, SLOTS, total), lambda j: (j, 0, 0)),
        ],
        out_specs=[pl.BlockSpec((n, 2 * width), lambda j: (0, j)) for width in widths],
        out_shape=[jax.ShapeDtypeStruct((n, width * CUTS), BF16) for width in widths],
        compiler_params=params(),
        cost_estimate=cost(2 * slots * n * total * CUTS, 2 * total * CUTS * (n + slots)),
    )(spots, moved)


def held_weights(w_ref, t):
    _, rank, width = w_ref.shape
    return w_ref[pl.ds(STEP * t, HELD)].reshape(HELD * rank, width)


def by_tile(kernel, ins, out, scratch, flops, whole_out=False):
    def spec(shape):
        if shape[1] == SLOTS:
            return pl.BlockSpec((shape[0], TILE, shape[2]), lambda t: (0, t, 0))
        return pl.BlockSpec(shape, lambda t: (0, 0, 0))

    moved = sum(v.size * v.dtype.itemsize for v in ins) + out.size * out.dtype.itemsize
    return pl.pallas_call(
        kernel,
        grid=(TILES,),
        in_specs=[spec(v.shape) for v in ins],
        out_specs=pl.BlockSpec(out.shape, lambda t: (0,) * len(out.shape)) if whole_out else spec(out.shape),
        out_shape=out,
        scratch_shapes=scratch,
        compiler_params=params(),
        cost_estimate=cost(flops, moved),
    )(*ins)


def part_kernel(rows, weights, part, compute):
    sources, _, width = rows.shape
    count, columns = sources * TILE, 128
    groups = sources // CUTS

    def kernel(me_ref, x_ref, w_ref, *refs):
        outs, held_ref = refs[:-1], refs[-1]
        t = pl.program_id(0)
        total = compute(x_ref[...].reshape(count, width), held_weights(w_ref, t), row_block(count, t))
        held_ref[...] = total.reshape(sources, TILE, columns)
        for r in range(CUTS):
            outs[r][...] = held_ref[pl.ds((me_ref[0] ^ r) * groups, groups)]

    moved = 2 * (rows.size + weights.size) + 4 * sources * SLOTS * columns
    return pl.pallas_call(
        kernel,
        grid=(TILES,),
        in_specs=[
            pl.BlockSpec(memory_space=pltpu.SMEM),
            pl.BlockSpec((sources, TILE, width), lambda t: (0, t, 0)),
            pl.BlockSpec(weights.shape, lambda t: (0, 0, 0)),
        ],
        out_specs=[pl.BlockSpec((groups, TILE, columns), lambda t: (0, t, 0))] * CUTS,
        out_shape=[jax.ShapeDtypeStruct((groups, SLOTS, columns), F32)] * CUTS,
        scratch_shapes=[pltpu.VMEM((sources, TILE, columns), F32)],
        compiler_params=params(),
        cost_estimate=cost(2 * TILES * count * HELD * weights.shape[1] * width, moved),
    )(part, rows, weights)


def lowered_part(rows, shrink, part):
    rank = shrink.shape[1]

    def compute(x, w, block):
        dense = lax.dot_general(x, w, (((1,), (1,)), ((), ())), preferred_element_type=F32)
        total = jnp.zeros((x.shape[0], rank), F32)
        for b in range(HELD):
            total = total + jnp.where(block == b, dense[:, b * rank : (b + 1) * rank], 0.0)
        return total

    return part_kernel(rows, shrink, part, compute)


def backward_part(rows, expand, split, part):
    width, rank = rows.shape[2], expand.shape[1]

    def compute(x, w, block):
        def half(lo, hi):
            dense = lax.dot_general(
                x[:, lo:hi], w[:, lo:hi], (((1,), (1,)), ((), ())), preferred_element_type=F32
            )
            total = jnp.zeros((x.shape[0], 2 * rank), F32)
            for p in range(HELD // 2):
                piece = dense[:, 2 * rank * p : 2 * rank * (p + 1)]
                total = total + jnp.where(pair_of(block, p), piece, 0.0)
            return total + pltpu.roll(total, rank, 1)

        first = iota((x.shape[0], 2 * rank), 1) < rank
        return jnp.where(first, half(0, split), half(split, width))

    return part_kernel(rows, expand, part, compute)


def join_sums(low, back):
    groups, slots, rank = low[0].shape

    def kernel(*refs):
        o_ref = refs[-1]
        for at, factor in ((0, 1.0), (1, SCALE)):
            total = refs[at * CUTS][...]
            for ref in refs[at * CUTS + 1 : (at + 1) * CUTS]:
                total = total + ref[...]
            o_ref[:, :, at * rank : (at + 1) * rank] = (factor * total).astype(BF16)

    return pl.pallas_call(
        kernel,
        out_shape=jax.ShapeDtypeStruct((groups, slots, 2 * rank), BF16),
        compiler_params=params(),
        cost_estimate=cost(2 * CUTS * low[0].size, 8 * CUTS * low[0].size),
        name="join_sums",
    )(*low, *back)


def spread_pairs(values, count, rank, t):
    held = values.reshape(count, 2 * rank).astype(F32)
    turned = pltpu.roll(held, rank, 1)
    first = iota((count, 2 * rank), 1) < rank
    halves = (jnp.where(first, held, turned), jnp.where(first, turned, held))
    block = row_block(count, t)
    return [
        jnp.concatenate(
            [jnp.where(pair_of(block, p), half, 0.0) for p in range(HELD // 2)], axis=1
        ).astype(BF16)
        for half in halves
    ]


def spread_blocks(values, count, rank, t):
    held = values.reshape(count, rank).astype(F32)
    block = row_block(count, t)
    return jnp.concatenate(
        [jnp.where(block == b, held, 0.0) for b in range(HELD)], axis=1
    ).astype(BF16)


def expand_rows(pieces, part, expand, split):
    groups, _, columns = pieces[0].shape
    sources = groups * CUTS
    count, rank, width = sources * TILE, expand.shape[1], expand.shape[2]

    def kernel(me_ref, *refs):
        ins, w_ref, o_ref, j_ref = refs[:CUTS], refs[CUTS], refs[-2], refs[-1]
        t = pl.program_id(0)
        for r in range(CUTS):
            j_ref[pl.ds((me_ref[0] ^ r) * groups, groups)] = ins[r][...]
        w = held_weights(w_ref, t)
        halves = spread_pairs(j_ref[:, :, : 2 * rank], count, rank, t)
        for half, lo, hi in zip(halves, (0, split), (split, width)):
            result = SCALE * jnp.dot(half, w[:, lo:hi], preferred_element_type=F32)
            o_ref[:, :, lo:hi] = result.astype(BF16).reshape(sources, TILE, hi - lo)

    return pl.pallas_call(
        kernel,
        grid=(TILES,),
        in_specs=[pl.BlockSpec(memory_space=pltpu.SMEM)]
        + [pl.BlockSpec((groups, TILE, columns), lambda t: (0, t, 0))] * CUTS
        + [pl.BlockSpec(expand.shape, lambda t: (0, 0, 0))],
        out_specs=[
            pl.BlockSpec((sources, TILE, width), lambda t: (0, t, 0)),
            pl.BlockSpec((sources, TILE, columns), lambda t: (0, t, 0)),
        ],
        out_shape=[
            jax.ShapeDtypeStruct((sources, SLOTS, width), BF16),
            jax.ShapeDtypeStruct((sources, SLOTS, columns), BF16),
        ],
        compiler_params=params(),
        cost_estimate=cost(
            2 * TILES * count * HELD * rank * width, 2 * (expand.size + sources * SLOTS * (width + 2 * columns))
        ),
        name="expand_rows",
    )(part, *pieces, expand)


def token_rows(joint, shrink):
    sources = joint.shape[0]
    count, rank, width = sources * TILE, shrink.shape[1], shrink.shape[2]

    def kernel(b_ref, w_ref, o_ref):
        t = pl.program_id(0)
        wide = spread_blocks(b_ref[:, :, rank:], count, rank, t)
        result = jnp.dot(wide, held_weights(w_ref, t), preferred_element_type=F32)
        o_ref[...] = result.astype(BF16).reshape(sources, TILE, width)

    return by_tile(
        kernel,
        (joint, shrink),
        jax.ShapeDtypeStruct((sources, SLOTS, width), BF16),
        [],
        2 * TILES * count * HELD * rank * width,
    )


def add_carry(carry_ref, pieces, rank, lo, hi):
    t = pl.program_id(0)
    first = pieces[:rank] + jnp.where(t > 0, carry_ref[:, lo:hi], 0.0)
    carry_ref[:, lo:hi] = pieces[STEP * rank :]
    done = jnp.concatenate([first, pieces[rank : STEP * rank]], axis=0)
    return done.astype(BF16).reshape(STEP, rank, hi - lo)


def fold(piece, width):
    narrow = piece.shape[-1]
    return jnp.concatenate([piece[..., 8 * i : 8 * i + 8, :] for i in range(width // narrow)], axis=-1)


def gradients(joint, rows_tokens, rows_both, split):
    sources, _, both = rows_both.shape
    count, pair = sources * TILE, joint.shape[2] // 2
    rank = pair // 2
    height = pair + rank + 8

    def put(o_ref, at, size, begin, end, value):
        o_ref[pl.ds(at, size), begin:end, :] = value

    def kernel(j_ref, t_ref, x_ref, o_ref, shrink_ref, expand_ref):
        t = pl.program_id(0)
        turn = (((0,), (0,)), ((), ()))
        wide = spread_blocks(j_ref[:, :, pair:], count, pair, t)
        tokens = t_ref[...].reshape(count, split)
        pieces = lax.dot_general(wide, tokens, turn, preferred_element_type=F32)
        put(o_ref, STEP * t, STEP, 0, pair, add_carry(shrink_ref, pieces, pair, 0, split))

        x = x_ref[...].reshape(count, both)
        halves = spread_pairs(j_ref[:, :, :pair], count, rank, t)
        pieces = SCALE * lax.dot_general(halves[0], x[:, :split], turn, preferred_element_type=F32)
        put(o_ref, STEP * t, STEP, pair, pair + rank, add_carry(expand_ref, pieces, rank, 0, split))
        pieces = SCALE * lax.dot_general(halves[1], x[:, split:], turn, preferred_element_type=F32)
        first = pieces[:rank] + jnp.where(t > 0, expand_ref[:, split:], 0.0)
        expand_ref[:, split:] = pieces[STEP * rank :]
        for b in range(STEP):
            piece = first if b == 0 else pieces[b * rank : (b + 1) * rank]
            o_ref[STEP * t + b, pair + rank :, :] = fold(piece, split).astype(BF16)

        @pl.when(t == TILES - 1)
        def _():
            o_ref[BLOCKS - 1, :pair, :] = shrink_ref[...].astype(BF16)
            o_ref[BLOCKS - 1, pair : pair + rank, :] = expand_ref[:, :split].astype(BF16)
            o_ref[BLOCKS - 1, pair + rank :, :] = fold(expand_ref[:, split:], split).astype(BF16)

    return by_tile(
        kernel,
        (joint, rows_tokens, rows_both),
        jax.ShapeDtypeStruct((BLOCKS, height, split), BF16),
        [pltpu.VMEM((pair, split), F32), pltpu.VMEM((rank, both), F32)],
        2 * TILES * count * HELD * (pair * split + rank * both),
        whole_out=True,
    )


def unpack(sums, rank, narrow):
    local, _, width = sums.shape
    pair = 2 * rank

    def kernel(g_ref, s_ref, q_ref, v_ref):
        s_ref[...] = g_ref[:, :pair, :].astype(F32)
        q_ref[...] = g_ref[:, pair : pair + rank, :].astype(F32)
        last = g_ref[:, pair + rank :, :].astype(F32)
        for i in range(width // narrow):
            v_ref[:, 8 * i : 8 * i + 8, :] = last[:, :, narrow * i : narrow * (i + 1)]

    return pl.pallas_call(
        kernel,
        out_shape=[
            jax.ShapeDtypeStruct((local, pair, width), F32),
            jax.ShapeDtypeStruct((local, rank, width), F32),
            jax.ShapeDtypeStruct((local, rank, narrow), F32),
        ],
        compiler_params=params(),
        cost_estimate=cost(sums.size, 6 * sums.size),
        name="unpack",
    )(sums)


ROUTE = ("y", "c", "x")
PARTS = ("y", "c")


def exchange(values):
    return lax.all_to_all(values, ROUTE, 0, 0, tiled=True)


def gathered(shard):
    return lax.all_gather(shard, "z", axis=0, tiled=True)


def summed(parts):
    return lax.psum_scatter(parts, "z", scatter_dimension=0, tiled=True)


def to_partners(parts):
    moved = [parts[0]]
    for r in range(1, CUTS):
        moved.append(lax.ppermute(parts[r], PARTS, [(i, i ^ r) for i in range(CUTS)]))
    return moved


def body(tokens, adapter_index, query_cotangent, value_cotangent, shrink, query_expand, value_expand):
    sources = lax.axis_size(ROUTE)
    local, kinds, rank, width = shrink.shape
    value_width = value_expand.shape[2]

    whole_shrink = gathered(shrink.reshape(local, kinds * rank, width))
    sent_tokens = place(adapter_index, (tokens,), sources)
    rows_tokens = exchange(sent_tokens)
    whole_expand = gathered(jnp.concatenate([query_expand, value_expand], axis=2))
    sent_both = place(adapter_index, (query_cotangent, value_cotangent), sources)
    rows_both = exchange(sent_both)

    spots = find_slots(adapter_index, sources // CUTS * SLOTS)
    me = jnp.reshape(lax.axis_index(PARTS), (1,)).astype(jnp.int32)
    low = to_partners(lowered_part(rows_tokens, whole_shrink, me))
    back = to_partners(backward_part(rows_both, whole_expand, width, me))
    pieces = to_partners([join_sums(low, back)] * CUTS)

    sent_both, joint = expand_rows(pieces, me, whole_expand, width)
    out_both = exchange(sent_both)
    sums = summed(gradients(joint, rows_tokens, rows_both, width))
    out_tokens = exchange(token_rows(joint, whole_shrink))

    query_delta, value_delta = collect(spots, out_both, (width, value_width))
    (token_gradient,) = collect(spots, out_tokens, (width,))
    grad_shrink, grad_query, grad_value = unpack(sums, rank, value_width)
    return (
        query_delta,
        value_delta,
        token_gradient,
        grad_shrink.reshape(local, kinds, rank, width),
        grad_query,
        grad_value,
    )


def solution(mesh):
    grid = Mesh(mesh.devices.reshape(4, 2, 4, 8), ("y", "c", "x", "z"))
    rows = P(("y", "c", "x", "z"), None)
    weights = (
        P(("x", "z"), None, None, PARTS),
        P(("x", "z"), None, PARTS),
        P(("x", "z"), None, PARTS),
    )

    return jax.shard_map(
        body,
        mesh=grid,
        in_specs=(rows, rows, rows, rows) + weights,
        out_specs=(rows, rows, rows) + weights,
        check_vma=False,
    )
```

```python
import jax
import jax.numpy as jnp
from jax import lax
from jax.experimental import pallas as pl
from jax.experimental.pallas import tpu as pltpu
from jax.sharding import Mesh, PartitionSpec as P


SCALE = 0.5
F32 = jnp.float32
BF16 = jnp.bfloat16
CAP = 3
CUTS = 8
BLOCKS = 16
SLOTS = BLOCKS * CAP
TILE = 16
TILES = SLOTS // TILE
STEP = 5
HELD = STEP + 1


def iota(shape, dim):
    return lax.broadcasted_iota(jnp.int32, shape, dim)


def cut_target(adapter, ordinal):
    return adapter * CAP + ordinal


def as_row(column):
    n = column.shape[0]
    return jnp.sum(jnp.where(iota((n, n), 0) == iota((n, n), 1), column, 0), axis=0, keepdims=True)


def target_row(adapter):
    n = adapter.shape[0]
    row = as_row(adapter)
    same = (adapter == row) & (iota((n, n), 0) < iota((n, n), 1))
    return cut_target(row, jnp.sum(same.astype(jnp.int32), axis=0, keepdims=True))


def target_column(adapter):
    n = adapter.shape[0]
    same = (adapter == as_row(adapter)) & (iota((n, n), 1) < iota((n, n), 0))
    return cut_target(adapter, jnp.sum(same.astype(jnp.int32), axis=1, keepdims=True))


def row_block(rows, t):
    inner = (iota((rows, 128), 0) & (TILE - 1)) + t
    block = jnp.zeros((rows, 128), jnp.int32)
    for k in range(1, HELD):
        block = block + (inner >= CAP * k).astype(jnp.int32)
    return block


def pair_of(block, pair):
    half = (iota(block.shape, 1) >= 64).astype(jnp.int32)
    return block == 2 * pair + half


def params():
    return pltpu.CompilerParams(vmem_limit_bytes=40 << 20)


def cost(flops, moved):
    return pl.CostEstimate(flops=flops, bytes_accessed=moved, transcendentals=0)


def place(adapter, values, sources):
    n = adapter.shape[0]
    widths = [v.shape[1] // CUTS for v in values]
    total = sum(widths)
    groups = sources // CUTS
    slots = groups * SLOTS

    def kernel(a_ref, *refs):
        ins, o_ref, p_ref = refs[:-2], refs[-2], refs[-1]

        @pl.when(pl.program_id(0) == 0)
        def _():
            spot = iota((slots, n), 0) == target_row(a_ref[...])
            p_ref[...] = spot.astype(F32).astype(BF16)

        at = 0
        for v_ref, width in zip(ins, widths):
            for k in range(2):
                moved = jnp.dot(
                    p_ref[...], v_ref[:, k * width : (k + 1) * width], preferred_element_type=F32
                )
                moved = moved.astype(BF16).reshape(groups, SLOTS, width)
                o_ref[k * groups : (k + 1) * groups, :, at : at + width] = moved
            at += width

    return pl.pallas_call(
        kernel,
        grid=(CUTS // 2,),
        in_specs=[pl.BlockSpec((n, 1), lambda j: (0, 0))]
        + [pl.BlockSpec((n, 2 * width), lambda j: (0, j)) for width in widths],
        out_specs=pl.BlockSpec((2 * groups, SLOTS, total), lambda j: (j, 0, 0)),
        out_shape=pltpu.HBM((sources, SLOTS, total), BF16),
        scratch_shapes=[pltpu.VMEM((slots, n), BF16)],
        compiler_params=params(),
        cost_estimate=cost(2 * slots * n * total * CUTS, 2 * total * CUTS * (n + slots)),
    )(adapter, *values)


def find_slots(adapter, slots):
    n = adapter.shape[0]

    def kernel(a_ref, o_ref):
        spot = iota((n, slots), 1) == target_column(a_ref[...])
        o_ref[...] = spot.astype(F32).astype(BF16)

    return pl.pallas_call(
        kernel,
        out_shape=jax.ShapeDtypeStruct((n, slots), BF16),
        compiler_params=params(),
        cost_estimate=cost(n * slots, 2 * n * slots),
        name="find_slots",
    )(adapter)


def collect(spots, moved, widths):
    n, slots = spots.shape
    sources, _, total = moved.shape
    groups = sources // CUTS

    def kernel(p_ref, m_ref, *outs):
        at = 0
        for o_ref, width in zip(outs, widths):
            for k in range(2):
                found = jnp.dot(
                    p_ref[...],
                    m_ref[k * groups : (k + 1) * groups, :, at : at + width].reshape(slots, width),
                    preferred_element_type=F32,
                )
                o_ref[:, k * width : (k + 1) * width] = found.astype(BF16)
            at += width

    return pl.pallas_call(
        kernel,
        grid=(CUTS // 2,),
        in_specs=[
            pl.BlockSpec((n, slots), lambda j: (0, 0)),
            pl.BlockSpec((2 * groups, SLOTS, total), lambda j: (j, 0, 0)),
        ],
        out_specs=[pl.BlockSpec((n, 2 * width), lambda j: (0, j)) for width in widths],
        out_shape=[jax.ShapeDtypeStruct((n, width * CUTS), BF16) for width in widths],
        compiler_params=params(),
        cost_estimate=cost(2 * slots * n * total * CUTS, 2 * total * CUTS * (n + slots)),
    )(spots, moved)


def held_weights(w_ref, t):
    _, rank, width = w_ref.shape
    return w_ref[pl.ds(STEP * t, HELD)].reshape(HELD * rank, width)


def by_tile(kernel, ins, out, scratch, flops, whole_out=False):
    def spec(shape):
        if shape[1] == SLOTS:
            return pl.BlockSpec((shape[0], TILE, shape[2]), lambda t: (0, t, 0))
        return pl.BlockSpec(shape, lambda t: (0, 0, 0))

    moved = sum(v.size * v.dtype.itemsize for v in ins) + out.size * out.dtype.itemsize
    return pl.pallas_call(
        kernel,
        grid=(TILES,),
        in_specs=[spec(v.shape) for v in ins],
        out_specs=pl.BlockSpec(out.shape, lambda t: (0,) * len(out.shape)) if whole_out else spec(out.shape),
        out_shape=pltpu.HBM(out.shape, out.dtype),
        scratch_shapes=scratch,
        compiler_params=params(),
        cost_estimate=cost(flops, moved),
    )(*ins)


def lowered_part(rows, shrink, part):
    sources, _, width = rows.shape
    count, rank = sources * TILE, shrink.shape[1]
    groups = sources // CUTS

    def kernel(me_ref, x_ref, w_ref, *refs):
        outs, held_ref = refs[:-1], refs[-1]
        t = pl.program_id(0)
        dense = lax.dot_general(
            x_ref[...].reshape(count, width),
            held_weights(w_ref, t),
            (((1,), (1,)), ((), ())),
            preferred_element_type=F32,
        )
        block = row_block(count, t)
        total = jnp.zeros((count, rank), F32)
        for b in range(HELD):
            total = total + jnp.where(block == b, dense[:, b * rank : (b + 1) * rank], 0.0)
        held_ref[...] = total.reshape(sources, TILE, rank)
        for r in range(CUTS):
            outs[r][...] = held_ref[pl.ds((me_ref[0] ^ r) * groups, groups)]

    moved = 2 * (rows.size + shrink.size) + 4 * sources * SLOTS * rank
    return pl.pallas_call(
        kernel,
        grid=(TILES,),
        in_specs=[
            pl.BlockSpec(memory_space=pltpu.SMEM),
            pl.BlockSpec((sources, TILE, width), lambda t: (0, t, 0)),
            pl.BlockSpec(shrink.shape, lambda t: (0, 0, 0)),
        ],
        out_specs=[pl.BlockSpec((groups, TILE, rank), lambda t: (0, t, 0))] * CUTS,
        out_shape=[jax.ShapeDtypeStruct((groups, SLOTS, rank), F32)] * CUTS,
        scratch_shapes=[pltpu.VMEM((sources, TILE, rank), F32)],
        compiler_params=params(),
        cost_estimate=cost(2 * TILES * count * HELD * rank * width, moved),
        name="lowered_part",
    )(part, rows, shrink)


def backward_part(rows, expand, split):
    sources, _, width = rows.shape
    count, rank = sources * TILE, expand.shape[1]

    def kernel(x_ref, w_ref, o_ref):
        t = pl.program_id(0)
        x = x_ref[...].reshape(count, width)
        w = held_weights(w_ref, t)
        block = row_block(count, t)

        def part(lo, hi):
            dense = lax.dot_general(
                x[:, lo:hi], w[:, lo:hi], (((1,), (1,)), ((), ())), preferred_element_type=F32
            )
            total = jnp.zeros((count, 2 * rank), F32)
            for p in range(HELD // 2):
                piece = dense[:, 2 * rank * p : 2 * rank * (p + 1)]
                total = total + jnp.where(pair_of(block, p), piece, 0.0)
            return total + pltpu.roll(total, rank, 1)

        first = iota((count, 2 * rank), 1) < rank
        both = jnp.where(first, part(0, split), part(split, width))
        o_ref[...] = both.reshape(sources, TILE, 2 * rank)

    return by_tile(
        kernel,
        (rows, expand),
        jax.ShapeDtypeStruct((sources, SLOTS, 2 * rank), F32),
        [],
        2 * TILES * count * HELD * rank * width,
    )


def join_sums(low, back):
    parts, count, rank = back.shape

    def kernel(*refs):
        ins, b_ref, o_ref = refs[:parts], refs[parts], refs[-1]
        total = ins[0][...]
        for ref in ins[1:]:
            total = total + ref[...]
        o_ref[:, :rank] = total.reshape(count, rank).astype(BF16)
        total = b_ref[0]
        for p in range(1, parts):
            total = total + b_ref[p]
        o_ref[:, rank:] = (SCALE * total).astype(BF16)

    return pl.pallas_call(
        kernel,
        out_shape=jax.ShapeDtypeStruct((count, 2 * rank), BF16),
        compiler_params=params(),
        cost_estimate=cost(2 * back.size, 8 * back.size),
        name="join_sums",
    )(*low, back)


def spread_pairs(values, count, rank, t):
    held = values.reshape(count, 2 * rank).astype(F32)
    turned = pltpu.roll(held, rank, 1)
    first = iota((count, 2 * rank), 1) < rank
    halves = (jnp.where(first, held, turned), jnp.where(first, turned, held))
    block = row_block(count, t)
    return [
        jnp.concatenate(
            [jnp.where(pair_of(block, p), half, 0.0) for p in range(HELD // 2)], axis=1
        ).astype(BF16)
        for half in halves
    ]


def spread_blocks(values, count, rank, t):
    held = values.reshape(count, rank).astype(F32)
    block = row_block(count, t)
    return jnp.concatenate(
        [jnp.where(block == b, held, 0.0) for b in range(HELD)], axis=1
    ).astype(BF16)


def expand_rows(joint, expand, split):
    sources = joint.shape[0]
    count, rank, width = sources * TILE, expand.shape[1], expand.shape[2]

    def kernel(l_ref, w_ref, o_ref):
        t = pl.program_id(0)
        w = held_weights(w_ref, t)
        halves = spread_pairs(l_ref[:, :, : 2 * rank], count, rank, t)
        for half, lo, hi in zip(halves, (0, split), (split, width)):
            result = SCALE * jnp.dot(half, w[:, lo:hi], preferred_element_type=F32)
            o_ref[:, :, lo:hi] = result.astype(BF16).reshape(sources, TILE, hi - lo)

    return by_tile(
        kernel,
        (joint, expand),
        jax.ShapeDtypeStruct((sources, SLOTS, width), BF16),
        [],
        2 * TILES * count * HELD * rank * width,
    )


def token_rows(joint, shrink):
    sources = joint.shape[0]
    count, rank, width = sources * TILE, shrink.shape[1], shrink.shape[2]

    def kernel(b_ref, w_ref, o_ref):
        t = pl.program_id(0)
        wide = spread_blocks(b_ref[:, :, rank:], count, rank, t)
        result = jnp.dot(wide, held_weights(w_ref, t), preferred_element_type=F32)
        o_ref[...] = result.astype(BF16).reshape(sources, TILE, width)

    return by_tile(
        kernel,
        (joint, shrink),
        jax.ShapeDtypeStruct((sources, SLOTS, width), BF16),
        [],
        2 * TILES * count * HELD * rank * width,
    )


def add_carry(carry_ref, pieces, rank, lo, hi):
    t = pl.program_id(0)
    first = pieces[:rank] + jnp.where(t > 0, carry_ref[:, lo:hi], 0.0)
    carry_ref[:, lo:hi] = pieces[STEP * rank :]
    done = jnp.concatenate([first, pieces[rank : STEP * rank]], axis=0)
    return done.astype(BF16).reshape(STEP, rank, hi - lo)


def fold(piece, width):
    narrow = piece.shape[-1]
    return jnp.concatenate([piece[..., 8 * i : 8 * i + 8, :] for i in range(width // narrow)], axis=-1)


def gradients(joint, rows_tokens, rows_both, split):
    sources, _, both = rows_both.shape
    count, pair = sources * TILE, joint.shape[2] // 2
    rank = pair // 2
    height = pair + rank + 8

    def put(o_ref, at, size, begin, end, value):
        o_ref[pl.ds(at, size), begin:end, :] = value

    def kernel(j_ref, t_ref, x_ref, o_ref, shrink_ref, expand_ref):
        t = pl.program_id(0)
        turn = (((0,), (0,)), ((), ()))
        wide = spread_blocks(j_ref[:, :, pair:], count, pair, t)
        tokens = t_ref[...].reshape(count, split)
        pieces = lax.dot_general(wide, tokens, turn, preferred_element_type=F32)
        put(o_ref, STEP * t, STEP, 0, pair, add_carry(shrink_ref, pieces, pair, 0, split))

        x = x_ref[...].reshape(count, both)
        halves = spread_pairs(j_ref[:, :, :pair], count, rank, t)
        pieces = SCALE * lax.dot_general(halves[0], x[:, :split], turn, preferred_element_type=F32)
        put(o_ref, STEP * t, STEP, pair, pair + rank, add_carry(expand_ref, pieces, rank, 0, split))
        pieces = SCALE * lax.dot_general(halves[1], x[:, split:], turn, preferred_element_type=F32)
        first = pieces[:rank] + jnp.where(t > 0, expand_ref[:, split:], 0.0)
        expand_ref[:, split:] = pieces[STEP * rank :]
        for b in range(STEP):
            piece = first if b == 0 else pieces[b * rank : (b + 1) * rank]
            o_ref[STEP * t + b, pair + rank :, :] = fold(piece, split).astype(BF16)

        @pl.when(t == TILES - 1)
        def _():
            o_ref[BLOCKS - 1, :pair, :] = shrink_ref[...].astype(BF16)
            o_ref[BLOCKS - 1, pair : pair + rank, :] = expand_ref[:, :split].astype(BF16)
            o_ref[BLOCKS - 1, pair + rank :, :] = fold(expand_ref[:, split:], split).astype(BF16)

    return by_tile(
        kernel,
        (joint, rows_tokens, rows_both),
        jax.ShapeDtypeStruct((BLOCKS, height, split), BF16),
        [pltpu.VMEM((pair, split), F32), pltpu.VMEM((rank, both), F32)],
        2 * TILES * count * HELD * (pair * split + rank * both),
        whole_out=True,
    )


def unpack(sums, rank, narrow):
    local, _, width = sums.shape
    pair = 2 * rank

    def kernel(g_ref, s_ref, q_ref, v_ref):
        s_ref[...] = g_ref[:, :pair, :].astype(F32)
        q_ref[...] = g_ref[:, pair : pair + rank, :].astype(F32)
        last = g_ref[:, pair + rank :, :].astype(F32)
        for i in range(width // narrow):
            v_ref[:, 8 * i : 8 * i + 8, :] = last[:, :, narrow * i : narrow * (i + 1)]

    return pl.pallas_call(
        kernel,
        out_shape=[
            jax.ShapeDtypeStruct((local, pair, width), F32),
            jax.ShapeDtypeStruct((local, rank, width), F32),
            jax.ShapeDtypeStruct((local, rank, narrow), F32),
        ],
        compiler_params=params(),
        cost_estimate=cost(sums.size, 6 * sums.size),
        name="unpack",
    )(sums)


ROUTE = ("y", "c", "x")
PARTS = ("y", "c")


def exchange(values):
    return lax.all_to_all(values, ROUTE, 0, 0, tiled=True)


def gathered(shard):
    return lax.all_gather(shard, "z", axis=0, tiled=True)


def summed(parts):
    return lax.psum_scatter(parts, "z", scatter_dimension=0, tiled=True)


def small_exchange(part):
    parts = lax.axis_size(PARTS)
    sources, slots, rank = part.shape
    return lax.all_to_all(part.reshape(parts, sources * slots // parts, rank), PARTS, 0, 0, tiled=True)


def body(tokens, adapter_index, query_cotangent, value_cotangent, shrink, query_expand, value_expand):
    sources = lax.axis_size(ROUTE)
    local, kinds, rank, width = shrink.shape
    value_width = value_expand.shape[2]

    whole_shrink = gathered(shrink.reshape(local, kinds * rank, width))
    sent_tokens = place(adapter_index, (tokens,), sources)
    rows_tokens = exchange(sent_tokens)
    whole_expand = gathered(jnp.concatenate([query_expand, value_expand], axis=2))
    sent_both = place(adapter_index, (query_cotangent, value_cotangent), sources)
    rows_both = exchange(sent_both)

    spots = find_slots(adapter_index, sources // CUTS * SLOTS)
    me = jnp.reshape(lax.axis_index(PARTS), (1,)).astype(jnp.int32)
    low = []
    for r, part in enumerate(lowered_part(rows_tokens, whole_shrink, me)):
        turns = [(i, i ^ r) for i in range(CUTS)]
        low.append(lax.ppermute(part, PARTS, turns) if r else part)
    back = small_exchange(backward_part(rows_both, whole_expand, width))
    joint = lax.all_gather(join_sums(low, back), PARTS, axis=0, tiled=True)
    joint = joint.reshape(sources, SLOTS, 4 * rank)

    out_both = exchange(expand_rows(joint, whole_expand, width))
    sums = summed(gradients(joint, rows_tokens, rows_both, width))
    out_tokens = exchange(token_rows(joint, whole_shrink))

    query_delta, value_delta = collect(spots, out_both, (width, value_width))
    (token_gradient,) = collect(spots, out_tokens, (width,))
    grad_shrink, grad_query, grad_value = unpack(sums, rank, value_width)
    return (
        query_delta,
        value_delta,
        token_gradient,
        grad_shrink.reshape(local, kinds, rank, width),
        grad_query,
        grad_value,
    )


def solution(mesh):
    grid = Mesh(mesh.devices.reshape(4, 2, 4, 8), ("y", "c", "x", "z"))
    rows = P(("y", "c", "x", "z"), None)
    weights = (
        P(("x", "z"), None, None, PARTS),
        P(("x", "z"), None, PARTS),
        P(("x", "z"), None, PARTS),
    )

    return jax.shard_map(
        body,
        mesh=grid,
        in_specs=(rows, rows, rows, rows) + weights,
        out_specs=(rows, rows, rows) + weights,
        check_vma=False,
    )
```
